32 devices in a mesh: fsdp: 8 (over y, x, core), seq: 4 (over z).
Axes of the slice: x: 2, y: 2, z: 4, core: 2. Of those that a mesh axis runs over, the one named last changes fastest.
Arguments:
- tokens: bfloat16 [8, 2048, 768], P('fsdp', 'seq'), may hold values from -6 to 6
- cotangent: bfloat16 [8, 2048, 768], P('fsdp', 'seq'), may hold values from -6 to 6
- w_qkv: bfloat16 [768, 2304], P(('fsdp', 'seq')), may hold values from -0.3125 to 0.3125
- b_qkv: bfloat16 [2304], P(('fsdp', 'seq')), may hold values from -1.796875 to 1.796875
- w_out: bfloat16 [768, 768], P(('fsdp', 'seq')), may hold values from -0.875 to 0.875
- b_out: bfloat16 [768], P(('fsdp', 'seq')), may hold values from -1.796875 to 1.796875
- w_up: bfloat16 [768, 3072], P(('fsdp', 'seq')), may hold values from -0.21875 to 0.21875
- b_up: bfloat16 [3072], P(('fsdp', 'seq')), may hold values from -1.796875 to 1.796875
- w_down: bfloat16 [3072, 768], P(('fsdp', 'seq')), may hold values from -0.109375 to 0.109375
- b_down: bfloat16 [768], P(('fsdp', 'seq')), may hold values from -1.796875 to 1.796875
- gain_attn: bfloat16 [768], P(('fsdp', 'seq')), may hold values from 0.099609375 to 1.8984375
- shift_attn: bfloat16 [768], P(('fsdp', 'seq')), may hold values from -1.796875 to 1.796875
- gain_mlp: bfloat16 [768], P(('fsdp', 'seq')), may hold values from 0.099609375 to 1.8984375
- shift_mlp: bfloat16 [768], P(('fsdp', 'seq')), may hold values from -1.796875 to 1.796875
Outputs:
- block_out: bfloat16 [8, 2048, 768], P('fsdp', 'seq')
- grad_tokens: bfloat16 [8, 2048, 768], P('fsdp', 'seq')
- grad_w_qkv: float32 [768, 2304], P(('fsdp', 'seq'))
- grad_b_qkv: float32 [2304], P(('fsdp', 'seq'))
- grad_w_out: float32 [768, 768], P(('fsdp', 'seq'))
- grad_b_out: float32 [768], P(('fsdp', 'seq'))
- grad_w_up: float32 [768, 3072], P(('fsdp', 'seq'))
- grad_b_up: float32 [3072], P(('fsdp', 'seq'))
- grad_w_down: float32 [3072, 768], P(('fsdp', 'seq'))
- grad_b_down: float32 [768], P(('fsdp', 'seq'))
- grad_gain_attn: float32 [768], P(('fsdp', 'seq'))
- grad_shift_attn: float32 [768], P(('fsdp', 'seq'))
- grad_gain_mlp: float32 [768], P(('fsdp', 'seq'))
- grad_shift_mlp: float32 [768], P(('fsdp', 'seq'))
The draws below stay inside these ranges and needn't reach their ends.
All inputs are finite; a program needn't handle non-finite values.
Results may differ from the reference program's by a relative error of at most 0.012.
The reference program's roundings to bfloat16 on the way count: a program that leaves them out, or rounds other values in their place, can miss the bound.
Values may be sent and summed in bfloat16 or wider, within the bound.
No kernel may reach another device: no remote copies, remote signals or barrier semaphores. Data moves between devices by JAX's collectives and lax.ppermute only.
A program may use at most 192 MiB of HBM per device.

```python
import math
import jax
import jax.numpy as jnp
from jax import lax

D = 768
HEADS = 12
HEAD = 64
ROT = 16
FF = 3072
LEN = 2048
SEQS = 8


def with_spikes(values, own_key, source, target, blocks, factor):
    def block_of(position):
        return (jnp.arange(values.shape[position]) // (values.shape[position] // blocks)).reshape((-1,) + (1,) * (values.ndim - 1 - position))

    one_side = jax.random.permutation(own_key, blocks)[block_of(target)]
    far = (block_of(target) + blocks // 2) % blocks
    return jnp.where((block_of(source) == one_side) | (block_of(source) == far), factor * values, values)


def steps_of(key, dims, shards, least, high):
    def one(axis_at, shards_of):
        steps = jax.random.uniform(jax.random.fold_in(jax.random.fold_in(key, 6), axis_at), (shards_of,), jnp.float32, least / len(shards), high / len(shards))
        return jnp.repeat(jnp.exp(steps), dims[axis_at] // shards_of).reshape((-1,) + (1,) * (len(dims) - axis_at - 1))

    factor_of = one(*shards[0])
    for cut in shards[1:]:
        factor_of = factor_of * one(*cut)
    return factor_of


def bell_draw(rng, dims, spread, bound, cuts=(), kind=jnp.bfloat16):
    values = jax.random.normal(rng, dims, jnp.float32) * spread
    if len(cuts) > 0:
        values = steps_of(rng, dims, cuts, -0.22, 0.18) * values
    return jnp.clip(values, min=-bound, max=bound).astype(kind)


def heavy_noise(rng, shape, spread, most, cuts, heavy, kind=jnp.bfloat16):
    values = spread * jax.random.normal(rng, shape, jnp.float32)
    if cuts:
        values = values * steps_of(rng, shape, cuts, -0.22, 0.18)
    return jnp.clip(with_spikes(values, jax.random.fold_in(rng, 3), *heavy), -most, most).astype(kind)


def setup_inputs(seed: int = 0) -> dict:
    key_list = jax.random.split(jax.random.key(seed), 15)
    return {
        "tokens": heavy_noise(key_list[0], (SEQS, LEN, D), 1.0, 6.0, ((0, 8), (1, 4)), (0, 2, 8, 2.0)),
        "cotangent": heavy_noise(key_list[1], (SEQS, LEN, D), 1.0, 6.0, ((0, 8), (1, 4)), (0, 2, 8, 2.0)),
        "w_qkv": bell_draw(key_list[2], (D, 3 * D), (D // 2) ** -0.5, 0.3125, ((0, 32),)),
        "b_qkv": bell_draw(key_list[3], (3 * D,), 0.3, 1.796875, ((0, 32),)),
        "w_out": bell_draw(key_list[4], (D, D), (D // 16) ** -0.5, 0.875, ((0, 32),)),
        "b_out": bell_draw(key_list[5], (D,), 0.3, 1.796875, ((0, 32),)),
        "w_up": bell_draw(key_list[6], (D, FF), D ** -0.5, 0.21875, ((0, 32),)),
        "b_up": bell_draw(key_list[7], (FF,), 0.3, 1.796875, ((0, 32),)),
        "w_down": bell_draw(key_list[8], (FF, D), FF ** -0.5, 0.109375, ((0, 32),)),
        "b_down": bell_draw(key_list[9], (D,), 0.3, 1.796875, ((0, 32),)),
        "gain_attn": jnp.clip(1.0 + 0.18 * jax.random.normal(key_list[10], (D,), jnp.float32), 0.099609375, 1.8984375).astype(jnp.bfloat16),
        "shift_attn": bell_draw(key_list[11], (D,), 0.3, 1.796875, ((0, 32),)),
        "gain_mlp": jnp.clip(1.0 + 0.18 * jax.random.normal(key_list[12], (D,), jnp.float32), 0.099609375, 1.8984375).astype(jnp.bfloat16),
        "shift_mlp": bell_draw(key_list[13], (D,), 0.3, 1.796875, ((0, 32),)),
    }


@jax.custom_vjp
def low(v):
    return lax.optimization_barrier(v.astype(jnp.bfloat16)).astype(jnp.float32)

@jax.custom_vjp
def low_back(v):
    return v

def low_keep(v):
    return (low(v), None)

def low_pass(kept, grad):
    return (grad,)

def back_keep(v):
    return (v, None)

def back_low(kept, grad):
    return (low(grad),)
low.defvjp(low_keep, low_pass)
low_back.defvjp(back_keep, back_low)
eps = 1e-05
mask_fill = -1e+30
highest = lax.Precision.HIGHEST

def layer_norm(inputs, gain_vec, shift_vec):
    row_mean = lax.optimization_barrier(jnp.mean(inputs, axis=-1, keepdims=True))
    centred = inputs - row_mean
    row_var = lax.optimization_barrier(jnp.mean(centred * centred, axis=-1, keepdims=True))
    return centred * lax.rsqrt(row_var + eps) * gain_vec + shift_vec

def rotary_tables(positions):
    half_rot = ROT // 2
    freq_index = jnp.arange(half_rot, dtype=jnp.int32).astype(jnp.float32)
    inv_freq = jnp.exp(freq_index * (-2.0 * math.log(10000.0) / ROT))
    angles = positions.astype(jnp.float32)[:, None] * inv_freq[None, :]
    return (jnp.cos(angles), jnp.sin(angles))

def rotate(heads_arr, cosine_tab, sine_tab):
    half_rot = ROT // 2
    first_half = heads_arr[..., :half_rot]
    second_half = heads_arr[..., half_rot:ROT]
    rest_part = heads_arr[..., ROT:]
    cos_wide = cosine_tab[:, None, :]
    sin_wide = sine_tab[:, None, :]
    return jnp.concatenate([first_half * cos_wide - second_half * sin_wide, second_half * cos_wide + first_half * sin_wide, rest_part], axis=-1)

def attend(queries, key_arr, value_arr):
    block_rows = min(512, LEN)
    score_scale = HEAD ** (-0.5)
    key_pos = jnp.arange(LEN, dtype=jnp.int32)

    def one_block(row_begin):
        query_blk = lax.dynamic_slice_in_dim(queries, row_begin, block_rows, 1)
        scores = jnp.einsum('gqhd,gkhd->ghqk', query_blk, key_arr, precision=highest) * score_scale
        scores = low_back(scores)
        query_pos = row_begin + jnp.arange(block_rows, dtype=jnp.int32)
        allowed = key_pos[None, :] <= query_pos[:, None]
        masked = jnp.where(allowed[None, None], scores, mask_fill)
        prob_low = low(jax.nn.softmax(masked, axis=-1))
        return jnp.einsum('ghqk,gkhd->gqhd', prob_low, value_arr, precision=highest)
    starts = (jnp.arange(LEN // block_rows, dtype=jnp.int32) * block_rows).astype(jnp.int32)
    blocks = lax.map(jax.checkpoint(one_block), starts)
    blocks = jnp.moveaxis(blocks, 0, 1)
    return blocks.reshape(queries.shape[0], LEN, HEADS * HEAD)

def block_forward(x_grp, w_qkv, b_qkv, w_out, b_out, w_up, b_up, w_down, b_down, gain_attn, shift_attn, gain_mlp, shift_mlp):
    seq_group = x_grp.shape[0]
    flat_x = x_grp.reshape(seq_group * LEN, D)
    normed_one = low(layer_norm(flat_x, gain_attn, shift_attn))
    normed_two = low(layer_norm(flat_x, gain_mlp, shift_mlp))
    projected = low_back(jnp.dot(normed_one, w_qkv, precision=highest) + b_qkv)
    parts = projected.reshape(seq_group, LEN, 3, HEADS, HEAD)
    cosine_tab, sine_tab = rotary_tables(jnp.arange(LEN, dtype=jnp.int32))
    query_rot = rotate(parts[:, :, 0], cosine_tab, sine_tab)
    key_rot = rotate(parts[:, :, 1], cosine_tab, sine_tab)
    turned = jnp.stack([query_rot, key_rot, parts[:, :, 2]], axis=2)
    turned = low(low_back(turned))
    mixed = attend(turned[:, :, 0], turned[:, :, 1], turned[:, :, 2])
    mixed = low(low_back(mixed)).reshape(seq_group * LEN, D)
    attn_out = jnp.dot(mixed, w_out, precision=highest) + b_out
    hidden_pre = low_back(jnp.dot(normed_two, w_up, precision=highest) + b_up)
    hidden = low(jax.nn.gelu(hidden_pre, approximate=False))
    mlp_out = jnp.dot(hidden, w_down, precision=highest) + b_down
    return (flat_x + attn_out + mlp_out).reshape(seq_group, LEN, D)

def reference(tokens, cotangent, w_qkv, b_qkv, w_out, b_out, w_up, b_up, w_down, b_down, gain_attn, shift_attn, gain_mlp, shift_mlp):
    params = tuple((member.astype(jnp.float32) for member in (w_qkv, b_qkv, w_out, b_out, w_up, b_up, w_down, b_down, gain_attn, shift_attn, gain_mlp, shift_mlp)))
    group_seqs = math.gcd(SEQS, max(1, 4096 // LEN))
    group_count = SEQS // group_seqs
    x_groups = tokens.astype(jnp.float32).reshape(group_count, group_seqs, LEN, D)
    cot_groups = cotangent.astype(jnp.float32).reshape(group_count, group_seqs, LEN, D)
    zero_grads = tuple((jnp.zeros_like(member) for member in params))

    def step_group(running, pair):
        x_grp, cot_grp = pair
        result, pullback = jax.vjp(block_forward, x_grp, *params)
        grads = pullback(cot_grp)
        updated = tuple((total + fresh for total, fresh in zip(running, grads[1:])))
        return (updated, (result.astype(jnp.bfloat16), grads[0].astype(jnp.bfloat16)))
    totals, (outputs, input_grads) = lax.scan(step_group, zero_grads, (x_groups, cot_groups))
    block_out = outputs.reshape(SEQS, LEN, D)
    grad_tokens = input_grads.reshape(SEQS, LEN, D)
    return (block_out, grad_tokens, totals[0], totals[1], totals[2], totals[3], totals[4], totals[5], totals[6], totals[7], totals[8], totals[9], totals[10], totals[11])
```

```python
import math

import jax
import jax.numpy as jnp
from jax import lax
from jax.experimental import pallas as pl
from jax.experimental.pallas import tpu as pltpu
from jax.sharding import PartitionSpec as P

HEAD = 64
ROT = 16
mask_fill = -1e30
eps = 1e-05
BLK = 256
F32 = jnp.float32
BF = jnp.bfloat16


def rot_tables(positions):
    lane = lax.broadcasted_iota(jnp.int32, (1, 128), 1) % HEAD
    half = ROT // 2
    inv = jnp.exp((lane % half).astype(F32) * (-2.0 * math.log(10000.0) / ROT))
    ang = positions.astype(F32)[:, None] * inv
    cos, sin = jnp.cos(ang), jnp.sin(ang)
    c = jnp.where(lane < ROT, cos, 1.0)
    sa = jnp.where(lane < half, -sin, 0.0)
    sb = jnp.where((lane >= half) & (lane < ROT), sin, 0.0)
    return c, sa, sb

def nt(a, b):
    return lax.dot_general(a, b, (((1,), (1,)), ((), ())), preferred_element_type=F32)

def nn(a, b):
    return lax.dot_general(a, b, (((1,), (0,)), ((), ())), preferred_element_type=F32)

def attend(rank, proj, grad_mixed, tables):
    n, c, width = grad_mixed.shape
    heads = width // HEAD
    length = n * c
    half = ROT // 2
    nq = length // BLK
    scale = HEAD ** (-0.5)

    def kernel(rank_ref, proj_ref, gm_ref, c_ref, sa_ref, sb_ref, mixed_ref, gp_ref, sum_ref,
               q_s, k_s, v_s, d_s, dk_s, dv_s, s_s, dp_s, p_s):
        rank = rank_ref[0]

        def spin(x, at, sign):
            cc, sa, sb = c_ref[at], sa_ref[at], sb_ref[at]
            left = pltpu.roll(x, 128 - half, 1)
            right = pltpu.roll(x, half, 1)
            return x * cc + sign * (left * sa + right * sb)

        def load(chunk, carry):
            at = lax.rem(rank - chunk + n, n)
            rows = pl.ds(pl.multiple_of(chunk * c, c), c)
            for tile in range(2 * width // 128):
                x = spin(proj_ref[at, :, tile * 128:(tile + 1) * 128], at, 1.0)
                for side in range(2):
                    slot = tile * 2 + side
                    piece = x[:, side * HEAD:(side + 1) * HEAD].astype(BF)
                    if slot < heads:
                        q_s[slot, rows, :] = piece * jnp.asarray(scale, BF)
                    else:
                        k_s[slot - heads, rows, :] = piece
            for h in range(heads):
                v_s[h, rows, :] = proj_ref[at, :, 2 * width + h * HEAD:2 * width + (h + 1) * HEAD].astype(BF)
                d_s[h, rows, :] = gm_ref[at, :, h * HEAD:(h + 1) * HEAD]
            return carry
        lax.fori_loop(0, n, load, 0)

        def one_head(h, carry):
            dk_s[h] = jnp.zeros((length, HEAD), F32)
            dv_s[h] = jnp.zeros((length, HEAD), F32)
            row = lax.broadcasted_iota(jnp.int32, (BLK, BLK), 0)
            col = lax.broadcasted_iota(jnp.int32, (BLK, BLK), 1)
            tri = row <= col
            for i in range(nq):
                span = slice(i * BLK, (i + 1) * BLK)
                qi = q_s[h, span, :]
                di = d_s[h, span, :]
                top = jnp.full((8, BLK), mask_fill, F32)
                for j in range(i + 1):
                    s = nt(k_s[h, j * BLK:(j + 1) * BLK, :], qi)
                    if j == i:
                        s = jnp.where(tri, s, mask_fill)
                    s_s[j] = s
                    top = jnp.maximum(top, jnp.max(s.reshape(BLK // 8, 8, BLK), axis=0))
                top = jnp.max(top, axis=0, keepdims=True)
                tot = jnp.zeros((8, BLK), F32)
                for j in range(i + 1):
                    e = jnp.exp(s_s[j] - top)
                    s_s[j] = e
                    tot = tot + jnp.sum(e.reshape(BLK // 8, 8, BLK), axis=0)
                inv = 1.0 / jnp.sum(tot, axis=0, keepdims=True)
                out = jnp.zeros((HEAD, BLK), F32)
                delta = jnp.zeros((8, BLK), F32)
                for j in range(i + 1):
                    keys = slice(j * BLK, (j + 1) * BLK)
                    p = s_s[j] * inv
                    s_s[j] = p
                    low = p.astype(BF)
                    dp = nt(v_s[h, keys, :], di)
                    dp_s[j] = dp
                    delta = delta + jnp.sum((p * dp).reshape(BLK // 8, 8, BLK), axis=0)
                    out = out + nn(v_s[h, keys, :].T, low)
                    dv_s[h, keys, :] = dv_s[h, keys, :] + nn(low, di)
                delta = jnp.sum(delta, axis=0, keepdims=True)
                dq = jnp.zeros((HEAD, BLK), F32)
                for j in range(i + 1):
                    keys = slice(j * BLK, (j + 1) * BLK)
                    ds = (s_s[j] * (dp_s[j] - delta)).astype(BF)
                    dq = dq + nn(k_s[h, keys, :].T, ds)
                    dk_s[h, keys, :] = dk_s[h, keys, :] + nn(ds, qi)
                q_s[h, span, :] = (dq * scale).T.astype(BF)
                d_s[h, span, :] = out.T.astype(BF)
            return carry
        lax.fori_loop(0, heads, one_head, 0)

        sum_ref[...] = jnp.zeros_like(sum_ref)

        def store(chunk, carry):
            at = lax.rem(rank - chunk + n, n)
            rows = pl.ds(pl.multiple_of(chunk * c, c), c)
            for tile in range(2 * width // 128):
                pieces = []
                for side in range(2):
                    slot = tile * 2 + side
                    if slot < heads:
                        pieces.append(q_s[slot, rows, :].astype(F32))
                    else:
                        pieces.append(dk_s[slot - heads, rows, :].astype(BF).astype(F32))
                x = spin(jnp.concatenate(pieces, axis=1), at, -1.0).astype(BF)
                lanes = slice(tile * 128, (tile + 1) * 128)
                gp_ref[at, :, lanes] = x
                sum_ref[:, lanes] += jnp.sum(x.astype(F32).reshape(c // 8, 8, 128), axis=0)
            x = jnp.concatenate([dv_s[h, rows, :].astype(BF) for h in range(heads)], axis=1)
            gp_ref[at, :, 2 * width:] = x
            sum_ref[:, 2 * width:] += jnp.sum(x.astype(F32).reshape(c // 8, 8, width), axis=0)
            mixed_ref[at] = jnp.concatenate([d_s[h, rows, :] for h in range(heads)], axis=1)
            return carry
        lax.fori_loop(0, n, store, 0)

    vm = pl.BlockSpec(memory_space=pltpu.VMEM)
    flops = 6 * heads * length * length * HEAD
    return pl.pallas_call(
        kernel,
        out_shape=(
            jax.ShapeDtypeStruct((n, c, width), BF),
            jax.ShapeDtypeStruct((n, c, 3 * width), BF),
            jax.ShapeDtypeStruct((8, 3 * width), F32),
        ),
        in_specs=[pl.BlockSpec(memory_space=pltpu.SMEM)] + [vm] * 5,
        out_specs=(vm, vm, vm),
        scratch_shapes=[pltpu.VMEM((heads, length, HEAD), BF)] * 4
        + [pltpu.VMEM((heads, length, HEAD), F32)] * 2
        + [pltpu.VMEM((nq, BLK, BLK), F32)] * 2 + [pltpu.VMEM((8, 128), BF)],
        compiler_params=pltpu.CompilerParams(vmem_limit_bytes=56 << 20),
        cost_estimate=pl.CostEstimate(flops=flops * 4, bytes_accessed=16 << 20, transcendentals=heads * length * length // 2),
        name="attend",
    )(rank, proj, grad_mixed, *tables)


def tn(a, b):
    return lax.dot_general(a, b, (((0,), (0,)), ((), ())), preferred_element_type=F32)


def make_body(nf, n):
    both = ("fsdp", "seq")

    def send(x, k):
        return lax.ppermute(x, "seq", [(i, (i + k) % n) for i in range(n)])

    def body(
        tokens,
        cotangent,
        w_qkv,
        b_qkv,
        w_out,
        b_out,
        w_up,
        b_up,
        w_down,
        b_down,
        gain_attn,
        shift_attn,
        gain_mlp,
        shift_mlp,
    ):
        rank = lax.axis_index("seq")
        _, c, d = tokens.shape
        rows = w_qkv.shape[0]
        width = d // n
        units = w_down.shape[0]
        tok = tokens.reshape(c, d)
        cot = cotangent.reshape(c, d)

        toks = [tok] + [send(tok, k) for k in range(1, n)]

        full_out = lax.all_gather(w_out, both, axis=0, tiled=True)
        qkv_cols = w_qkv.reshape(rows, 3, n, width).transpose(2, 0, 1, 3).reshape(n, rows, 3 * width)
        up_cols = w_up.reshape(rows, nf, n, units).transpose(2, 0, 1, 3).reshape(n, rows, nf * units)
        cols = jnp.concatenate([qkv_cols, up_cols], axis=2)
        cols = lax.all_to_all(cols, "seq", split_axis=0, concat_axis=0, tiled=True)
        cols = lax.all_gather(cols.reshape(n * rows, -1), "fsdp", axis=0, tiled=True)
        own_qkv = cols[:, : 3 * width]
        own_up = cols[:, 3 * width :]
        own_down = lax.all_gather(w_down, "fsdp", axis=0, tiled=True)

        vectors = (b_qkv, b_out, b_up, b_down, gain_attn, shift_attn, gain_mlp, shift_mlp)
        lengths = [v.shape[0] for v in vectors]
        pad = -sum(lengths) % 1024
        pack = jnp.concatenate(vectors + (jnp.zeros((pad,), BF),)).reshape(-1, 128)
        packs = lax.all_gather(pack, both, axis=0, tiled=True).reshape(nf * n, -1)
        full = []
        at = 0
        for size in lengths:
            full.append(packs[:, at : at + size].reshape(-1).astype(F32))
            at += size
        bias_qkv, bias_out, bias_up, bias_down, gain_one, shift_one, gain_two, shift_two = full
        own_bias_qkv = lax.dynamic_index_in_dim(
            bias_qkv.reshape(3, n, width), rank, 1, keepdims=False
        ).reshape(-1)
        own_bias_up = lax.dynamic_index_in_dim(
            bias_up.reshape(nf, n, units), rank, 1, keepdims=False
        ).reshape(-1)

        out_blocks = [
            lax.dynamic_slice_in_dim(full_out, (rank + k) % n * width, width, 0) for k in range(n)
        ]
        grad_mixed = []
        for k in range(n):
            part = nt(cot, out_blocks[k]).astype(BF)
            grad_mixed.append(send(part, k) if k else part)

        late_cot, toks[-1] = lax.optimization_barrier((cot, toks[-1]))
        cots = [cot] + [send(late_cot, k) for k in range(1, n)]

        hats, ones, twos, scales, projected = [], [], [], [], []
        for k in range(n):
            x = toks[k].astype(F32)
            centred = x - jnp.mean(x, axis=-1, keepdims=True)
            spread = lax.rsqrt(jnp.mean(centred * centred, axis=-1, keepdims=True) + eps)
            hat = centred * spread
            hats.append(hat)
            scales.append(spread)
            ones.append((hat * gain_one + shift_one).astype(BF))
            twos.append((hat * gain_two + shift_two).astype(BF))
            projected.append(nn(ones[k], own_qkv) + own_bias_qkv)
        tables = [
            [t for t in rot_tables(((rank - k) % n) * c + jnp.arange(c, dtype=jnp.int32))]
            for k in range(n)
        ]
        tables = [jnp.stack(t) for t in zip(*tables)]

        pres, hiddens = [], []
        mlp_out = None
        for k in range(n):
            pre = nn(twos[k], own_up) + own_bias_up
            hidden = jax.nn.gelu(pre, approximate=False).astype(BF)
            pres.append(pre)
            hiddens.append(hidden)
            part = nn(hidden, own_down)
            part = send(part.astype(BF), -k).astype(F32) if k else part
            mlp_out = part if mlp_out is None else mlp_out + part

        mixed, grad_proj, sum_qkv = attend(
            jnp.full((1,), rank, jnp.int32), jnp.stack(projected), jnp.stack(grad_mixed), tables
        )

        cot_float = cot.astype(F32)
        grad_pres, incoming = [], []
        sum_up = sum_gain_two = sum_shift_two = 0.0
        for k in range(n):
            grad_hidden = nt(cots[k], own_down)
            pre = pres[k]
            slope = 0.5 * (1.0 + lax.erf(pre * math.sqrt(0.5))) + pre * jnp.exp(
                -0.5 * pre * pre
            ) * (1.0 / math.sqrt(2.0 * math.pi))
            grad_pre = (grad_hidden * slope).astype(BF)
            grad_pres.append(grad_pre)
            sum_up += jnp.sum(grad_pre.astype(F32), axis=0)
            arriving = nt(grad_pre, own_up)
            sum_gain_two += jnp.sum(arriving * hats[k], axis=0)
            sum_shift_two += jnp.sum(arriving, axis=0)
            incoming.append(arriving * gain_two)
        hidden_all = jnp.concatenate(hiddens)
        cot_all = jnp.concatenate(cots)
        one_all = jnp.concatenate(ones)
        two_all = jnp.concatenate(twos)
        grad_down = tn(hidden_all, cot_all)
        grad_up = tn(two_all, jnp.concatenate(grad_pres))

        def reduce_rows(grad):
            return lax.psum_scatter(grad.astype(BF), "fsdp", scatter_dimension=0, tiled=True)

        def to_owners(grad):
            grad = reduce_rows(grad).reshape(n, rows, -1)
            return lax.all_to_all(grad, "seq", split_axis=0, concat_axis=0, tiled=True).astype(F32)

        grad_w_down = reduce_rows(grad_down).astype(F32)
        grad_w_up = (
            to_owners(grad_up).reshape(n, rows, nf, units).transpose(1, 2, 0, 3).reshape(rows, -1)
        )

        attn_out = None
        grad_out = jnp.zeros((n, width, d), F32)
        for k in range(n):
            part = send(mixed[k], -k) if k else mixed[k]
            term = nn(part, out_blocks[k])
            attn_out = term if attn_out is None else attn_out + term
            grad_out = lax.dynamic_update_index_in_dim(grad_out, tn(part, cot), (rank + k) % n, 0)
        block_out = tok.astype(F32) + attn_out + bias_out + mlp_out + bias_down
        grad_w_out = lax.psum_scatter(
            grad_out.reshape(d, d).astype(BF), both, scatter_dimension=0, tiled=True
        ).astype(F32)

        grad_q = None
        sum_gain_one = sum_shift_one = 0.0
        for k in range(n):
            arriving = nt(grad_proj[k], own_qkv)
            sum_gain_one += jnp.sum(arriving * hats[k], axis=0)
            sum_shift_one += jnp.sum(arriving, axis=0)
            part = arriving * gain_one + incoming[k]
            part = send(part.astype(BF), -k).astype(F32) if k else part
            grad_q = part if grad_q is None else grad_q + part
        grad_qkv = tn(one_all, grad_proj.reshape(n * c, -1))
        grad_w_qkv = (
            to_owners(grad_qkv).reshape(n, rows, 3, width).transpose(1, 2, 0, 3).reshape(rows, -1)
        )
        grad_tokens = cot_float + scales[0] * (
            grad_q
            - jnp.mean(grad_q, axis=-1, keepdims=True)
            - hats[0] * jnp.mean(grad_q * hats[0], axis=-1, keepdims=True)
        )

        def place(values, parts):
            blank = jnp.zeros((parts, n, values.size // parts), F32)
            filled = lax.dynamic_update_index_in_dim(blank, values.reshape(parts, -1), rank, 1)
            return filled.reshape(-1)

        sum_out = jnp.sum(cot_float, axis=0)
        sums = (
            place(jnp.sum(sum_qkv, axis=0), 3),
            sum_out,
            place(sum_up, nf),
            sum_out,
            sum_gain_one,
            sum_shift_one,
            sum_gain_two,
            sum_shift_two,
        )
        packed = jnp.concatenate(
            [s.reshape(nf * n, -1) for s in sums] + [jnp.zeros((nf * n, pad), F32)], axis=1
        )
        packed = lax.psum_scatter(
            packed.reshape(-1, 128), both, scatter_dimension=0, tiled=True
        ).reshape(-1)
        grads = []
        at = 0
        for size in lengths:
            grads.append(packed[at : at + size])
            at += size

        return (
            block_out.astype(BF).reshape(tokens.shape),
            grad_tokens.astype(BF).reshape(tokens.shape),
            grad_w_qkv,
            grads[0],
            grad_w_out,
            grads[1],
            grad_w_up,
            grads[2],
            grad_w_down,
            grads[3],
            grads[4],
            grads[5],
            grads[6],
            grads[7],
        )

    return body


def solution(mesh):
    tok = P("fsdp", "seq", None)
    mat = P(("fsdp", "seq"), None)
    vec = P(("fsdp", "seq"))
    params = (mat, vec, mat, vec, mat, vec, mat, vec, vec, vec, vec, vec)
    return jax.shard_map(
        make_body(mesh.shape["fsdp"], mesh.shape["seq"]),
        mesh=mesh,
        in_specs=(tok, tok) + params,
        out_specs=(tok, tok) + params,
        check_vma=False,
    )
```

```python
import math

import jax
import jax.numpy as jnp
from jax import lax
from jax.experimental import pallas as pl
from jax.experimental.pallas import tpu as pltpu
from jax.sharding import PartitionSpec as P

HEAD = 64
ROT = 16
mask_fill = -1e30
eps = 1e-05
BLK = 256
F32 = jnp.float32
BF = jnp.bfloat16


def rot_tables(positions):
    lane = lax.broadcasted_iota(jnp.int32, (1, 128), 1) % HEAD
    half = ROT // 2
    inv = jnp.exp((lane % half).astype(F32) * (-2.0 * math.log(10000.0) / ROT))
    ang = positions.astype(F32)[:, None] * inv
    cos, sin = jnp.cos(ang), jnp.sin(ang)
    c = jnp.where(lane < ROT, cos, 1.0)
    sa = jnp.where(lane < half, -sin, 0.0)
    sb = jnp.where((lane >= half) & (lane < ROT), sin, 0.0)
    return c, sa, sb

def nt(a, b):
    return lax.dot_general(a, b, (((1,), (1,)), ((), ())), preferred_element_type=F32)

def nn(a, b):
    return lax.dot_general(a, b, (((1,), (0,)), ((), ())), preferred_element_type=F32)

def attend(rank, proj, grad_mixed, tables):
    n, c, width = grad_mixed.shape
    heads = width // HEAD
    length = n * c
    half = ROT // 2
    nq = length // BLK
    scale = HEAD ** (-0.5)

    def kernel(rank_ref, proj_ref, gm_ref, c_ref, sa_ref, sb_ref, mixed_ref, gp_ref, sum_ref,
               q_s, k_s, v_s, d_s, dk_s, dv_s, s_s, dp_s, p_s):
        rank = rank_ref[0]

        def spin(x, at, sign):
            cc, sa, sb = c_ref[at], sa_ref[at], sb_ref[at]
            left = pltpu.roll(x, 128 - half, 1)
            right = pltpu.roll(x, half, 1)
            return x * cc + sign * (left * sa + right * sb)

        def load(chunk, carry):
            at = lax.rem(rank - chunk + n, n)
            rows = pl.ds(pl.multiple_of(chunk * c, c), c)
            for tile in range(2 * width // 128):
                x = spin(proj_ref[at, :, tile * 128:(tile + 1) * 128], at, 1.0)
                for side in range(2):
                    slot = tile * 2 + side
                    piece = x[:, side * HEAD:(side + 1) * HEAD].astype(BF)
                    if slot < heads:
                        q_s[slot, rows, :] = piece * jnp.asarray(scale, BF)
                    else:
                        k_s[slot - heads, rows, :] = piece
            for h in range(heads):
                v_s[h, rows, :] = proj_ref[at, :, 2 * width + h * HEAD:2 * width + (h + 1) * HEAD].astype(BF)
                d_s[h, rows, :] = gm_ref[at, :, h * HEAD:(h + 1) * HEAD]
            return carry
        lax.fori_loop(0, n, load, 0)

        def one_head(h, carry):
            dk_s[h] = jnp.zeros((length, HEAD), F32)
            dv_s[h] = jnp.zeros((length, HEAD), F32)
            row = lax.broadcasted_iota(jnp.int32, (BLK, BLK), 0)
            col = lax.broadcasted_iota(jnp.int32, (BLK, BLK), 1)
            tri = row <= col
            for i in range(nq):
                span = slice(i * BLK, (i + 1) * BLK)
                qi = q_s[h, span, :]
                di = d_s[h, span, :]
                top = jnp.full((8, BLK), mask_fill, F32)
                for j in range(i + 1):
                    s = nt(k_s[h, j * BLK:(j + 1) * BLK, :], qi)
                    if j == i:
                        s = jnp.where(tri, s, mask_fill)
                    s_s[j] = s
                    top = jnp.maximum(top, jnp.max(s.reshape(BLK // 8, 8, BLK), axis=0))
                top = jnp.max(top, axis=0, keepdims=True)
                tot = jnp.zeros((8, BLK), F32)
                for j in range(i + 1):
                    e = jnp.exp(s_s[j] - top)
                    s_s[j] = e
                    tot = tot + jnp.sum(e.reshape(BLK // 8, 8, BLK), axis=0)
                inv = 1.0 / jnp.sum(tot, axis=0, keepdims=True)
                out = jnp.zeros((HEAD, BLK), F32)
                delta = jnp.zeros((8, BLK), F32)
                for j in range(i + 1):
                    keys = slice(j * BLK, (j + 1) * BLK)
                    p = s_s[j] * inv
                    s_s[j] = p
                    low = p.astype(BF)
                    dp = nt(v_s[h, keys, :], di)
                    dp_s[j] = dp
                    delta = delta + jnp.sum((p * dp).reshape(BLK // 8, 8, BLK), axis=0)
                    out = out + nn(v_s[h, keys, :].T, low)
                    dv_s[h, keys, :] = dv_s[h, keys, :] + nn(low, di)
                delta = jnp.sum(delta, axis=0, keepdims=True)
                dq = jnp.zeros((HEAD, BLK), F32)
                for j in range(i + 1):
                    keys = slice(j * BLK, (j + 1) * BLK)
                    ds = (s_s[j] * (dp_s[j] - delta)).astype(BF)
                    dq = dq + nn(k_s[h, keys, :].T, ds)
                    dk_s[h, keys, :] = dk_s[h, keys, :] + nn(ds, qi)
                q_s[h, span, :] = (dq * scale).T.astype(BF)
                d_s[h, span, :] = out.T.astype(BF)
            return carry
        lax.fori_loop(0, heads, one_head, 0)

        sum_ref[...] = jnp.zeros_like(sum_ref)

        def store(chunk, carry):
            at = lax.rem(rank - chunk + n, n)
            rows = pl.ds(pl.multiple_of(chunk * c, c), c)
            for tile in range(2 * width // 128):
                pieces = []
                for side in range(2):
                    slot = tile * 2 + side
                    if slot < heads:
                        pieces.append(q_s[slot, rows, :].astype(F32))
                    else:
                        pieces.append(dk_s[slot - heads, rows, :].astype(BF).astype(F32))
                x = spin(jnp.concatenate(pieces, axis=1), at, -1.0).astype(BF)
                lanes = slice(tile * 128, (tile + 1) * 128)
                gp_ref[at, :, lanes] = x
                sum_ref[:, lanes] += jnp.sum(x.astype(F32).reshape(c // 8, 8, 128), axis=0)
            x = jnp.concatenate([dv_s[h, rows, :].astype(BF) for h in range(heads)], axis=1)
            gp_ref[at, :, 2 * width:] = x
            sum_ref[:, 2 * width:] += jnp.sum(x.astype(F32).reshape(c // 8, 8, width), axis=0)
            mixed_ref[at] = jnp.concatenate([d_s[h, rows, :] for h in range(heads)], axis=1)
            return carry
        lax.fori_loop(0, n, store, 0)

    vm = pl.BlockSpec(memory_space=pltpu.VMEM)
    flops = 6 * heads * length * length * HEAD
    return pl.pallas_call(
        kernel,
        out_shape=(
            jax.ShapeDtypeStruct((n, c, width), BF),
            jax.ShapeDtypeStruct((n, c, 3 * width), BF),
            jax.ShapeDtypeStruct((8, 3 * width), F32),
        ),
        in_specs=[pl.BlockSpec(memory_space=pltpu.SMEM)] + [vm] * 5,
        out_specs=(vm, vm, vm),
        scratch_shapes=[pltpu.VMEM((heads, length, HEAD), BF)] * 4
        + [pltpu.VMEM((heads, length, HEAD), F32)] * 2
        + [pltpu.VMEM((nq, BLK, BLK), F32)] * 2 + [pltpu.VMEM((8, 128), BF)],
        compiler_params=pltpu.CompilerParams(vmem_limit_bytes=56 << 20),
        cost_estimate=pl.CostEstimate(flops=flops * 4, bytes_accessed=16 << 20, transcendentals=heads * length * length // 2),
        name="attend",
    )(rank, proj, grad_mixed, *tables)


def tn(a, b):
    return lax.dot_general(a, b, (((0,), (0,)), ((), ())), preferred_element_type=F32)


def make_body(nf, n):
    both = ("fsdp", "seq")

    def send(x, k):
        return lax.ppermute(x, "seq", [(i, (i + k) % n) for i in range(n)])

    def hop(x, pairs):
        return lax.ppermute(x, "seq", pairs)

    def gather_ring(x, rank):
        right, left = [x], [x]
        for t in range(1, n):
            right.append(hop(right[-1], [(i, i + 1) for i in range(t - 1, n - 1)]))
            left.append(hop(left[-1], [(i, i - 1) for i in range(1, n - t + 1)]))
        return [x] + [jnp.where(rank >= k, right[k], left[n - k]) for k in range(1, n)]

    def scatter_ring(parts):
        right = left = None
        for t in range(1, n):
            rising = parts[t] if right is None else parts[t] + right.astype(F32)
            falling = parts[n - t] if left is None else parts[n - t] + left.astype(F32)
            right = hop(rising.astype(BF), [(i, i + 1) for i in range(t)])
            left = hop(falling.astype(BF), [(i, i - 1) for i in range(n - t, n)])
        return parts[0] + (right.astype(F32) + left.astype(F32))

    def body(
        tokens,
        cotangent,
        w_qkv,
        b_qkv,
        w_out,
        b_out,
        w_up,
        b_up,
        w_down,
        b_down,
        gain_attn,
        shift_attn,
        gain_mlp,
        shift_mlp,
    ):
        rank = lax.axis_index("seq")
        _, c, d = tokens.shape
        rows = w_qkv.shape[0]
        width = d // n
        units = w_down.shape[0]
        extra = 1
        while n * (rows + extra) % 16:
            extra += 1
        tok = tokens.reshape(c, d)
        cot = cotangent.reshape(c, d)

        toks = gather_ring(tok, rank)

        vectors = (b_qkv, b_out, b_up, b_down, gain_attn, shift_attn, gain_mlp, shift_mlp)
        lengths = [v.shape[0] for v in vectors]
        total = sum(lengths)
        pack = jnp.pad(jnp.concatenate(vectors).reshape(1, total), ((0, extra - 1), (0, d - total)))
        qkv_cols = w_qkv.reshape(rows, 3, n, width).transpose(2, 0, 1, 3).reshape(n, rows, 3 * width)
        up_cols = w_up.reshape(rows, nf, n, units).transpose(2, 0, 1, 3).reshape(n, rows, nf * units)
        cols = jnp.pad(jnp.concatenate([qkv_cols, up_cols], axis=2), ((0, 0), (0, extra), (0, 0)))
        same = jnp.broadcast_to(jnp.concatenate([w_out, pack])[None], (n, rows + extra, d))
        sent = jnp.concatenate([same, cols], axis=2)
        sent = lax.all_to_all(sent, "seq", split_axis=0, concat_axis=0, tiled=True)
        first = lax.all_gather(sent[:, :, :d].reshape(-1, d), "fsdp", axis=0, tiled=True)
        first = first.reshape(nf, n, rows + extra, d)
        full_out = first[:, :, :rows].reshape(d, d)
        packs = first[:, :, rows, :total].reshape(nf * n, total)
        cols = sent[:, :rows, d:].reshape(n * rows, -1)
        cols = lax.all_gather(cols, "fsdp", axis=0, tiled=True)
        own_qkv = cols[:, : 3 * width]
        own_up = cols[:, 3 * width :]
        own_down = lax.all_gather(w_down, "fsdp", axis=0, tiled=True)

        full = []
        at = 0
        for size in lengths:
            full.append(packs[:, at : at + size].reshape(-1).astype(F32))
            at += size
        bias_qkv, bias_out, bias_up, bias_down, gain_one, shift_one, gain_two, shift_two = full
        own_bias_qkv = lax.dynamic_index_in_dim(
            bias_qkv.reshape(3, n, width), rank, 1, keepdims=False
        ).reshape(-1)
        own_bias_up = lax.dynamic_index_in_dim(
            bias_up.reshape(nf, n, units), rank, 1, keepdims=False
        ).reshape(-1)

        out_blocks = [
            lax.dynamic_slice_in_dim(full_out, (rank + k) % n * width, width, 0) for k in range(n)
        ]
        grad_mixed = []
        for k in range(n):
            part = nt(cot, out_blocks[k]).astype(BF)
            grad_mixed.append(send(part, k) if k else part)

        late_cot, toks[-1] = lax.optimization_barrier((cot, toks[-1]))
        cots = gather_ring(late_cot, rank)

        hats, ones, twos, scales, projected = [], [], [], [], []
        for k in range(n):
            x = toks[k].astype(F32)
            centred = x - jnp.mean(x, axis=-1, keepdims=True)
            spread = lax.rsqrt(jnp.mean(centred * centred, axis=-1, keepdims=True) + eps)
            hat = centred * spread
            hats.append(hat)
            scales.append(spread)
            ones.append((hat * gain_one + shift_one).astype(BF))
            twos.append((hat * gain_two + shift_two).astype(BF))
            projected.append(nn(ones[k], own_qkv) + own_bias_qkv)
        tables = [
            [t for t in rot_tables(((rank - k) % n) * c + jnp.arange(c, dtype=jnp.int32))]
            for k in range(n)
        ]
        tables = [jnp.stack(t) for t in zip(*tables)]

        pres, hiddens = [], []
        mlp_parts = []
        for k in range(n):
            pre = nn(twos[k], own_up) + own_bias_up
            hidden = jax.nn.gelu(pre, approximate=False).astype(BF)
            pres.append(pre)
            hiddens.append(hidden)
            mlp_parts.append(nn(hidden, own_down))
        mlp_out = scatter_ring(mlp_parts)

        mixed, grad_proj, sum_qkv = attend(
            jnp.full((1,), rank, jnp.int32), jnp.stack(projected), jnp.stack(grad_mixed), tables
        )

        cot_float = cot.astype(F32)
        grad_pres, incoming = [], []
        sum_up = sum_gain_two = sum_shift_two = 0.0
        for k in range(n):
            grad_hidden = nt(cots[k], own_down)
            pre = pres[k]
            slope = 0.5 * (1.0 + lax.erf(pre * math.sqrt(0.5))) + pre * jnp.exp(
                -0.5 * pre * pre
            ) * (1.0 / math.sqrt(2.0 * math.pi))
            grad_pre = (grad_hidden * slope).astype(BF)
            grad_pres.append(grad_pre)
            sum_up += jnp.sum(grad_pre.astype(F32), axis=0)
            arriving = nt(grad_pre, own_up)
            sum_gain_two += jnp.sum(arriving * hats[k], axis=0)
            sum_shift_two += jnp.sum(arriving, axis=0)
            incoming.append(arriving * gain_two)
        hidden_all = jnp.concatenate(hiddens)
        cot_all = jnp.concatenate(cots)
        one_all = jnp.concatenate(ones)
        two_all = jnp.concatenate(twos)
        grad_down = tn(hidden_all, cot_all)
        grad_up = tn(two_all, jnp.concatenate(grad_pres))

        def reduce_rows(grad):
            return lax.psum_scatter(grad.astype(BF), "fsdp", scatter_dimension=0, tiled=True)

        def to_owners(grad):
            grad = reduce_rows(grad).reshape(n, -1, grad.shape[1])
            return lax.all_to_all(grad, "seq", split_axis=0, concat_axis=0, tiled=True).astype(F32)

        grad_w_down = reduce_rows(grad_down).astype(F32)
        grad_w_up = (
            to_owners(grad_up).reshape(n, rows, nf, units).transpose(1, 2, 0, 3).reshape(rows, -1)
        )

        attn_out = None
        for k in range(n):
            part = send(mixed[k], -k) if k else mixed[k]
            term = nn(part, out_blocks[k])
            attn_out = term if attn_out is None else attn_out + term
        block_out = tok.astype(F32) + attn_out + bias_out + mlp_out + bias_down
        grad_out = reduce_rows(tn(mixed.reshape(n * c, width), cot_all))
        grad_w_out = lax.ppermute(
            grad_out, both, [(f * n + s, s * nf + f) for f in range(nf) for s in range(n)]
        ).astype(F32)

        grad_q_parts = []
        sum_gain_one = sum_shift_one = 0.0
        for k in range(n):
            arriving = nt(grad_proj[k], own_qkv)
            sum_gain_one += jnp.sum(arriving * hats[k], axis=0)
            sum_shift_one += jnp.sum(arriving, axis=0)
            grad_q_parts.append(arriving * gain_one + incoming[k])
        grad_q = scatter_ring(grad_q_parts)
        grad_qkv = tn(one_all, grad_proj.reshape(n * c, -1))
        grad_tokens = cot_float + scales[0] * (
            grad_q
            - jnp.mean(grad_q, axis=-1, keepdims=True)
            - hats[0] * jnp.mean(grad_q * hats[0], axis=-1, keepdims=True)
        )

        def place(values, parts):
            blank = jnp.zeros((parts, n, values.size // parts), F32)
            filled = lax.dynamic_update_index_in_dim(blank, values.reshape(parts, -1), rank, 1)
            return filled.reshape(-1)

        sum_out = jnp.sum(cot_float, axis=0)
        sums = (
            place(jnp.sum(sum_qkv, axis=0), 3),
            sum_out,
            place(sum_up, nf),
            sum_out,
            sum_gain_one,
            sum_shift_one,
            sum_gain_two,
            sum_shift_two,
        )
        packed = jnp.concatenate([s.reshape(nf * n, -1) for s in sums], axis=1)
        packed = packed.reshape(nf, n, 1, total)
        packed = jnp.pad(packed, ((0, 0), (0, 0), (0, extra - 1), (0, 3 * width - total)))
        tail = jnp.concatenate([grad_qkv.reshape(nf, n, rows, 3 * width), packed], axis=2)
        tail = to_owners(tail.reshape(-1, 3 * width))
        grad_w_qkv = (
            tail[:, :rows].reshape(n, rows, 3, width).transpose(1, 2, 0, 3).reshape(rows, -1)
        )
        packed = jnp.sum(tail[:, rows], axis=0)
        grads = []
        at = 0
        for size in lengths:
            grads.append(packed[at : at + size])
            at += size

        return (
            block_out.astype(BF).reshape(tokens.shape),
            grad_tokens.astype(BF).reshape(tokens.shape),
            grad_w_qkv,
            grads[0],
            grad_w_out,
            grads[1],
            grad_w_up,
            grads[2],
            grad_w_down,
            grads[3],
            grads[4],
            grads[5],
            grads[6],
            grads[7],
        )

    return body


def solution(mesh):
    tok = P("fsdp", "seq", None)
    mat = P(("fsdp", "seq"), None)
    vec = P(("fsdp", "seq"))
    params = (mat, vec, mat, vec, mat, vec, mat, vec, vec, vec, vec, vec)
    return jax.shard_map(
        make_body(mesh.shape["fsdp"], mesh.shape["seq"]),
        mesh=mesh,
        in_specs=(tok, tok) + params,
        out_specs=(tok, tok) + params,
        check_vma=False,
    )
```

```python
import math

import jax
import jax.numpy as jnp
from jax import lax
from jax.experimental import pallas as pl
from jax.experimental.pallas import tpu as pltpu
from jax.sharding import PartitionSpec as P

HEAD = 64
ROT = 16
mask_fill = -1e30
eps = 1e-05
BLK = 256
F32 = jnp.float32
BF = jnp.bfloat16


def rot_tables(positions):
    lane = lax.broadcasted_iota(jnp.int32, (1, 128), 1) % HEAD
    half = ROT // 2
    inv = jnp.exp((lane % half).astype(F32) * (-2.0 * math.log(10000.0) / ROT))
    ang = positions.astype(F32)[:, None] * inv
    cos, sin = jnp.cos(ang), jnp.sin(ang)
    c = jnp.where(lane < ROT, cos, 1.0)
    sa = jnp.where(lane < half, -sin, 0.0)
    sb = jnp.where((lane >= half) & (lane < ROT), sin, 0.0)
    return c, sa, sb

def nt(a, b):
    return lax.dot_general(a, b, (((1,), (1,)), ((), ())), preferred_element_type=F32)

def nn(a, b):
    return lax.dot_general(a, b, (((1,), (0,)), ((), ())), preferred_element_type=F32)

def attend(rank, proj, grad_mixed, tables):
    n, c, width = grad_mixed.shape
    heads = width // HEAD
    length = n * c
    half = ROT // 2
    nq = length // BLK
    scale = HEAD ** (-0.5)

    def kernel(rank_ref, proj_ref, gm_ref, c_ref, sa_ref, sb_ref, mixed_ref, gp_ref, sum_ref,
               q_s, k_s, v_s, d_s, dk_s, dv_s, s_s, dp_s, p_s):
        rank = rank_ref[0]

        def spin(x, at, sign):
            cc, sa, sb = c_ref[at], sa_ref[at], sb_ref[at]
            left = pltpu.roll(x, 128 - half, 1)
            right = pltpu.roll(x, half, 1)
            return x * cc + sign * (left * sa + right * sb)

        def load(chunk, carry):
            at = lax.rem(rank - chunk + n, n)
            rows = pl.ds(pl.multiple_of(chunk * c, c), c)
            for tile in range(2 * width // 128):
                x = spin(proj_ref[at, :, tile * 128:(tile + 1) * 128], at, 1.0)
                for side in range(2):
                    slot = tile * 2 + side
                    piece = x[:, side * HEAD:(side + 1) * HEAD].astype(BF)
                    if slot < heads:
                        q_s[slot, rows, :] = piece * jnp.asarray(scale, BF)
                    else:
                        k_s[slot - heads, rows, :] = piece
            for h in range(heads):
                v_s[h, rows, :] = proj_ref[at, :, 2 * width + h * HEAD:2 * width + (h + 1) * HEAD].astype(BF)
                d_s[h, rows, :] = gm_ref[at, :, h * HEAD:(h + 1) * HEAD]
            return carry
        lax.fori_loop(0, n, load, 0)

        def one_head(h, carry):
            dk_s[h] = jnp.zeros((length, HEAD), F32)
            dv_s[h] = jnp.zeros((length, HEAD), F32)
            row = lax.broadcasted_iota(jnp.int32, (BLK, BLK), 0)
            col = lax.broadcasted_iota(jnp.int32, (BLK, BLK), 1)
            tri = row <= col
            for i in range(nq):
                span = slice(i * BLK, (i + 1) * BLK)
                qi = q_s[h, span, :]
                di = d_s[h, span, :]
                top = jnp.full((8, BLK), mask_fill, F32)
                for j in range(i + 1):
                    s = nt(k_s[h, j * BLK:(j + 1) * BLK, :], qi)
                    if j == i:
                        s = jnp.where(tri, s, mask_fill)
                    s_s[j] = s
                    top = jnp.maximum(top, jnp.max(s.reshape(BLK // 8, 8, BLK), axis=0))
                top = jnp.max(top, axis=0, keepdims=True)
                tot = jnp.zeros((8, BLK), F32)
                for j in range(i + 1):
                    e = jnp.exp(s_s[j] - top)
                    s_s[j] = e
                    tot = tot + jnp.sum(e.reshape(BLK // 8, 8, BLK), axis=0)
                inv = 1.0 / jnp.sum(tot, axis=0, keepdims=True)
                out = jnp.zeros((HEAD, BLK), F32)
                delta = jnp.zeros((8, BLK), F32)
                for j in range(i + 1):
                    keys = slice(j * BLK, (j + 1) * BLK)
                    p = s_s[j] * inv
                    s_s[j] = p
                    low = p.astype(BF)
                    dp = nt(v_s[h, keys, :], di)
                    dp_s[j] = dp
                    delta = delta + jnp.sum((p * dp).reshape(BLK // 8, 8, BLK), axis=0)
                    out = out + nn(v_s[h, keys, :].T, low)
                    dv_s[h, keys, :] = dv_s[h, keys, :] + nn(low, di)
                delta = jnp.sum(delta, axis=0, keepdims=True)
                dq = jnp.zeros((HEAD, BLK), F32)
                for j in range(i + 1):
                    keys = slice(j * BLK, (j + 1) * BLK)
                    ds = (s_s[j] * (dp_s[j] - delta)).astype(BF)
                    dq = dq + nn(k_s[h, keys, :].T, ds)
                    dk_s[h, keys, :] = dk_s[h, keys, :] + nn(ds, qi)
                q_s[h, span, :] = (dq * scale).T.astype(BF)
                d_s[h, span, :] = out.T.astype(BF)
            return carry
        lax.fori_loop(0, heads, one_head, 0)

        sum_ref[...] = jnp.zeros_like(sum_ref)

        def store(chunk, carry):
            at = lax.rem(rank - chunk + n, n)
            rows = pl.ds(pl.multiple_of(chunk * c, c), c)
            for tile in range(2 * width // 128):
                pieces = []
                for side in range(2):
                    slot = tile * 2 + side
                    if slot < heads:
                        pieces.append(q_s[slot, rows, :].astype(F32))
                    else:
                        pieces.append(dk_s[slot - heads, rows, :].astype(BF).astype(F32))
                x = spin(jnp.concatenate(pieces, axis=1), at, -1.0).astype(BF)
                lanes = slice(tile * 128, (tile + 1) * 128)
                gp_ref[at, :, lanes] = x
                sum_ref[:, lanes] += jnp.sum(x.astype(F32).reshape(c // 8, 8, 128), axis=0)
            x = jnp.concatenate([dv_s[h, rows, :].astype(BF) for h in range(heads)], axis=1)
            gp_ref[at, :, 2 * width:] = x
            sum_ref[:, 2 * width:] += jnp.sum(x.astype(F32).reshape(c // 8, 8, width), axis=0)
            mixed_ref[at] = jnp.concatenate([d_s[h, rows, :] for h in range(heads)], axis=1)
            return carry
        lax.fori_loop(0, n, store, 0)

    vm = pl.BlockSpec(memory_space=pltpu.VMEM)
    flops = 6 * heads * length * length * HEAD
    return pl.pallas_call(
        kernel,
        out_shape=(
            jax.ShapeDtypeStruct((n, c, width), BF),
            jax.ShapeDtypeStruct((n, c, 3 * width), BF),
            jax.ShapeDtypeStruct((8, 3 * width), F32),
        ),
        in_specs=[pl.BlockSpec(memory_space=pltpu.SMEM)] + [vm] * 5,
        out_specs=(vm, vm, vm),
        scratch_shapes=[pltpu.VMEM((heads, length, HEAD), BF)] * 4
        + [pltpu.VMEM((heads, length, HEAD), F32)] * 2
        + [pltpu.VMEM((nq, BLK, BLK), F32)] * 2 + [pltpu.VMEM((8, 128), BF)],
        compiler_params=pltpu.CompilerParams(vmem_limit_bytes=56 << 20),
        cost_estimate=pl.CostEstimate(flops=flops, bytes_accessed=16 << 20, transcendentals=heads * length * length // 2),
        name="attend",
    )(rank, proj, grad_mixed, *tables)


def tn(a, b):
    return lax.dot_general(a, b, (((0,), (0,)), ((), ())), preferred_element_type=F32)


def normalized(x):
    centred = x - jnp.mean(x, axis=-1, keepdims=True)
    spread = lax.rsqrt(jnp.mean(centred * centred, axis=-1, keepdims=True) + eps)
    return centred * spread, spread


def half_erf(pre):
    return 0.5 * (1.0 + lax.erf(pre * math.sqrt(0.5)))


def tokens_spec(size):
    return pl.BlockSpec((None, BLK, size), lambda i, j: (i, j, 0))


def whole_spec(shape):
    return pl.BlockSpec(shape, lambda i, j: (0,) * len(shape))


def rows8(v):
    return jnp.sum(v.reshape(BLK // 8, 8, v.shape[1]), axis=0)


def spread_out(ref, totals, nf):
    tall, d = ref.shape[1:]
    for f in range(nf):
        at = 0
        for total in totals:
            size, wide = total.shape[0] // nf, total.shape[1]
            ref[f, at : at + size, :wide] = total[f * size : (f + 1) * size, :].astype(BF)
            if wide < d:
                ref[f, at : at + size, wide:] = jnp.zeros((size, d - wide), BF)
            at += size
        if at < tall:
            ref[f, at:, :] = jnp.zeros((tall - at, d), BF)


def feed(nf, spare, toks, cots, norms, weights, b_qkv, w_out, b_up):
    n, c, d = toks.shape
    wide, width, hid = b_qkv.shape[1], w_out.shape[0], b_up.shape[1]
    last = n * (c // BLK) - 1
    tall = (d + hid) // nf + spare

    def kernel(
        x_ref, cot_ref, norm_ref, w_ref, bq_ref, wo_ref, bu_ref,
        proj_ref, mixed_ref, out_ref, q_ref, all_ref, sum_ref, up_ref, au, ad,
    ):
        w_up = w_ref[:, :hid]
        w_down = w_ref[:, hid : hid + d]
        w_qkv = w_ref[:, hid + d :]
        step = pl.program_id(0) * (c // BLK) + pl.program_id(1)

        @pl.when(step == 0)
        def _():
            for ref in (au, ad, sum_ref, up_ref):
                ref[...] = jnp.zeros_like(ref)

        hat, _ = normalized(x_ref[...].astype(F32))
        one = (hat * norm_ref[0:1] + norm_ref[1:2]).astype(BF)
        two = (hat * norm_ref[2:3] + norm_ref[3:4]).astype(BF)
        cot = cot_ref[...]
        proj_ref[...] = nn(one, w_qkv) + bq_ref[...]
        mixed_ref[...] = nt(cot, wo_ref[...]).astype(BF)
        pre = nn(two, w_up) + bu_ref[...]
        bell = half_erf(pre)
        hidden = (pre * bell).astype(BF)
        out_ref[...] = nn(hidden, w_down).astype(BF)
        slope = bell + pre * jnp.exp(-0.5 * pre * pre) * (1.0 / math.sqrt(2.0 * math.pi))
        grad_pre = (nt(cot, w_down) * slope).astype(BF)
        arriving = nt(grad_pre, w_up)
        q_ref[...] = (arriving * norm_ref[2:3]).astype(BF)
        sum_ref[0] += rows8(arriving * hat)
        sum_ref[1] += rows8(arriving)
        up_ref[...] += rows8(grad_pre.astype(F32))
        ad[...] += tn(hidden, cot)
        au[...] += tn(two, grad_pre)

        @pl.when(step == last)
        def _():
            spread_out(all_ref, (ad, au), nf)

    ins = (toks, cots, norms, weights, b_qkv, w_out, b_up)
    return pl.pallas_call(
        kernel,
        grid=(n, c // BLK),
        in_specs=[tokens_spec(d)] * 2 + [whole_spec(a.shape) for a in ins[2:]],
        out_specs=(
            tokens_spec(wide), tokens_spec(width), tokens_spec(d), tokens_spec(d),
            whole_spec((nf, tall, d)), whole_spec((2, 8, d)), whole_spec((8, hid)),
        ),
        out_shape=(
            jax.ShapeDtypeStruct((n, c, wide), F32),
            jax.ShapeDtypeStruct((n, c, width), BF),
            jax.ShapeDtypeStruct((n, c, d), BF),
            jax.ShapeDtypeStruct((n, c, d), BF),
            jax.ShapeDtypeStruct((nf, tall, d), BF),
            jax.ShapeDtypeStruct((2, 8, d), F32),
            jax.ShapeDtypeStruct((8, hid), F32),
        ),
        scratch_shapes=[pltpu.VMEM((d, hid), F32), pltpu.VMEM((hid, d), F32)],
        compiler_params=pltpu.CompilerParams(vmem_limit_bytes=60 << 20),
        cost_estimate=pl.CostEstimate(
            flops=2 * n * c * d * (wide + width + 6 * hid), bytes_accessed=30 << 20,
            transcendentals=2 * n * c * hid,
        ),
        name="feed",
    )(*ins)


def finish(nf, tall, toks, cots, rest, grad_proj, mixed, norms, weights):
    n, c, d = toks.shape
    wide, width = grad_proj.shape[2], mixed.shape[2]
    last = n * (c // BLK) - 1

    def kernel(
        x_ref, cot_ref, rest_ref, gp_ref, mixed_ref, norm_ref, wq_ref,
        q_ref, all_ref, sum_ref, aq, ao,
    ):
        step = pl.program_id(0) * (c // BLK) + pl.program_id(1)

        @pl.when(step == 0)
        def _():
            for ref in (aq, ao, sum_ref):
                ref[...] = jnp.zeros_like(ref)

        hat, _ = normalized(x_ref[...].astype(F32))
        one = (hat * norm_ref[0:1] + norm_ref[1:2]).astype(BF)
        grad_proj = gp_ref[...]
        arriving = nt(grad_proj, wq_ref[:, wq_ref.shape[1] - wide :])
        q_ref[...] = (arriving * norm_ref[0:1] + rest_ref[...].astype(F32)).astype(BF)
        sum_ref[0] += rows8(arriving * hat)
        sum_ref[1] += rows8(arriving)
        aq[...] += tn(one, grad_proj)
        ao[...] += tn(mixed_ref[...], cot_ref[...])

        @pl.when(step == last)
        def _():
            spread_out(all_ref, (aq, ao), nf)

    ins = (toks, cots, rest, grad_proj, mixed, norms, weights)
    return pl.pallas_call(
        kernel,
        grid=(n, c // BLK),
        in_specs=[tokens_spec(a.shape[2]) for a in ins[:5]] + [whole_spec(a.shape) for a in ins[5:]],
        out_specs=(tokens_spec(d), whole_spec((nf, tall, d)), whole_spec((2, 8, d))),
        out_shape=(
            jax.ShapeDtypeStruct((n, c, d), BF),
            jax.ShapeDtypeStruct((nf, tall, d), BF),
            jax.ShapeDtypeStruct((2, 8, d), F32),
        ),
        scratch_shapes=[pltpu.VMEM((d, wide), F32), pltpu.VMEM((width, d), F32)],
        compiler_params=pltpu.CompilerParams(vmem_limit_bytes=60 << 20),
        cost_estimate=pl.CostEstimate(
            flops=n * c * d, bytes_accessed=n * c * d, transcendentals=0
        ),
        name="finish",
    )(*ins)


def make_body(nf, n):
    both = ("fsdp", "seq")

    def send(x, k):
        return lax.ppermute(x, "seq", [(i, (i + k) % n) for i in range(n)])

    def hop(x, pairs):
        return lax.ppermute(x, "seq", pairs)

    def gather_ring(x, rank, between):
        right, left = [x], [x]
        for t in range(1, n):
            right[-1], left[-1] = between(t, (right[-1], left[-1]))
            right.append(hop(right[-1], [(i, i + 1) for i in range(t - 1, n - 1)]))
            left.append(hop(left[-1], [(i, i - 1) for i in range(1, n - t + 1)]))
        return [x] + [jnp.where(rank >= k, right[k], left[n - k]) for k in range(1, n)]

    def scatter_direct(parts):
        return [parts[0]] + [send(parts[k], -k) for k in range(1, n)]

    def scatter_ring(parts, between):
        right = left = None
        for t in range(1, n):
            if t == n - 1:
                between((right, left))
            rising = parts[t] if right is None else parts[t].astype(F32) + right.astype(F32)
            falling = parts[n - t] if left is None else parts[n - t].astype(F32) + left.astype(F32)
            right = hop(rising.astype(BF), [(i, i + 1) for i in range(t)])
            left = hop(falling.astype(BF), [(i, i - 1) for i in range(n - t, n)])
        return parts[0].astype(F32) + (right.astype(F32) + left.astype(F32))

    def in_order(parts, rank):
        out = jnp.zeros((n,) + parts[0].shape, parts[0].dtype)
        for k in range(n):
            out = lax.dynamic_update_index_in_dim(out, parts[k], (rank - k) % n, 0)
        return out

    def exchange(blocks, rank):
        own = [lax.dynamic_index_in_dim(blocks, (rank + k) % n, 0, keepdims=False) for k in range(n)]
        return in_order([send(own[k], k) if k else own[k] for k in range(n)], rank)

    def body(
        tokens,
        cotangent,
        w_qkv,
        b_qkv,
        w_out,
        b_out,
        w_up,
        b_up,
        w_down,
        b_down,
        gain_attn,
        shift_attn,
        gain_mlp,
        shift_mlp,
    ):
        rank = lax.axis_index("seq")
        _, c, d = tokens.shape
        rows = w_qkv.shape[0]
        width = d // n
        wide = 3 * width
        units = w_down.shape[0]
        extra = 8
        while n * (rows + extra) % 16:
            extra += 1
        tok = tokens.reshape(c, d)
        cot = cotangent.reshape(c, d)

        vectors = (b_qkv, b_out, b_up, b_down, gain_attn, shift_attn, gain_mlp, shift_mlp)
        lengths = [v.shape[0] for v in vectors]
        total = sum(lengths)
        pack = jnp.stack([jnp.pad(v, (0, d - v.shape[0])) for v in vectors])
        same = jnp.concatenate([w_out, pack, jnp.zeros((extra - len(vectors), d), BF)])
        qkv_cols = w_qkv.reshape(rows, 3, n, width).transpose(2, 0, 1, 3).reshape(n, rows, wide)
        up_cols = w_up.reshape(rows, nf, n, units).transpose(2, 0, 1, 3).reshape(n, rows, nf * units)
        message = jnp.concatenate(
            [
                jnp.broadcast_to(same, (n, rows + extra, d)),
                jnp.pad(up_cols, ((0, 0), (0, extra), (0, 0))),
                jnp.pad(qkv_cols, ((0, 0), (0, extra), (0, 0))),
            ],
            axis=2,
        )
        message = exchange(message, rank)
        hid = nf * units
        side = message[:, :rows, d:].reshape(n * rows, -1)
        second = jnp.concatenate([side[:, :hid], w_down, side[:, hid:]], axis=1)
        found = []

        def prepare():
            blocks = found[0].reshape(nf, n, rows + extra, d)
            full_out = blocks[:, :, :rows].reshape(d, d)
            full = [
                blocks[:, :, rows + i, :size].reshape(-1).astype(F32)
                for i, size in enumerate(lengths)
            ]
            norms = jnp.stack(full[4:] + [jnp.zeros((d,), F32)] * 4)
            own_bias_qkv = lax.dynamic_index_in_dim(full[0].reshape(3, n, width), rank, 1)
            own_bias_up = lax.dynamic_index_in_dim(full[2].reshape(nf, n, units), rank, 1)
            out_blocks = [
                lax.dynamic_slice_in_dim(full_out, (rank + k) % n * width, width, 0) for k in range(n)
            ]
            return (
                full[1] + full[3], norms, own_bias_qkv.reshape(1, -1), own_bias_up.reshape(1, -1),
                out_blocks,
            )

        def between(t, passed):
            if t == 2:
                tables = [
                    rot_tables((rank - k) % n * c + jnp.arange(c, dtype=jnp.int32)) for k in range(n)
                ]
                tables = [jnp.stack(t) for t in zip(*tables)]
                mine, tables, _ = lax.optimization_barrier((message[:, :, :d], tables, passed))
                mine = mine.reshape(n * (rows + extra), d)
                found.append(lax.all_gather(mine, "fsdp", axis=0, tiled=True))
                mine, _ = lax.optimization_barrier((second, passed))
                found.append(lax.all_gather(mine, "fsdp", axis=0, tiled=True))
                found.append(tables)
            if t == n - 1:
                ready, passed = lax.optimization_barrier((prepare(), passed))
                found.append(ready)
            return passed

        chunks = gather_ring(jnp.stack([tok, cot]), rank, between)
        toks = jnp.stack([pair[0] for pair in chunks])
        cots = jnp.stack([pair[1] for pair in chunks])
        _, weights, tables, (bias_ends, norms, own_bias_qkv, own_bias_up, out_blocks) = found

        def packed_row(sums, sizes):
            row = jnp.concatenate([v.reshape(nf, n, size) for v, size in zip(sums, sizes)], axis=2)
            row = row.reshape(nf, 1, n * sum(sizes)).astype(BF)
            return jnp.pad(row, ((0, 0), (0, 0), (0, d - row.shape[2])))

        def place(values, parts):
            mine = lax.broadcasted_iota(jnp.int32, (1, n, 1), 1) == rank
            return jnp.where(mine, values.reshape(parts, 1, -1), 0.0).reshape(-1)

        cot_float = cot.astype(F32)
        sum_out = jnp.sum(cot_float, axis=0)
        projected, grad_mixed, mlp_parts, rest, joined, sums_two, sum_up = feed(
            nf, -(-(2 * units + 1) // 16) * 16 - 2 * units, toks, cots, norms, weights,
            own_bias_qkv, out_blocks[0], own_bias_up,
        )
        mlp_parts = scatter_direct([mlp_parts[k] for k in range(n)])
        sums_two = jnp.sum(sums_two, axis=1)
        sizes = (lengths[1], lengths[2], lengths[3], lengths[6], lengths[7])
        row = packed_row(
            (sum_out, place(jnp.sum(sum_up, axis=0), nf), sum_out, sums_two[0], sums_two[1]), sizes
        )
        joined = lax.dynamic_update_slice(joined, row, (0, 2 * units, 0))
        joined = lax.psum_scatter(joined.reshape(-1, d), "fsdp", scatter_dimension=0, tiled=True)
        mixed, grad_proj, sum_qkv = attend(
            jnp.full((1,), rank, jnp.int32), projected, grad_mixed, tables
        )
        joined, mixed, grad_proj = lax.optimization_barrier((joined, mixed, grad_proj))
        mixed_own = [send(mixed[k], -k) if k else mixed[k] for k in range(n)]
        grad_w_down = joined[:units].astype(F32)
        filled = n * rows + rows
        tall = -(-(filled + 1) // 16) * 16
        grad_q, tail, sums_one = finish(
            nf, tall, toks, cots, rest, grad_proj, mixed, norms, weights
        )
        mlp_parts, grad_q, tail = lax.optimization_barrier((mlp_parts, grad_q, tail))

        sums_one = jnp.sum(sums_one, axis=1)
        late = (lengths[0], lengths[4], lengths[5])
        row = packed_row((place(jnp.sum(sum_qkv, axis=0), 3), sums_one[0], sums_one[1]), late)
        tail = lax.dynamic_update_slice(tail, row, (0, filled, 0))
        tail = lax.psum_scatter(tail.reshape(-1, d), "fsdp", scatter_dimension=0, tiled=True)
        grad_w_out = lax.ppermute(
            tail[n * rows : filled],
            both,
            [(f * n + s, s * nf + f) for f in range(nf) for s in range(n)],
        ).astype(F32)

        def to_owners(block, line, sizes):
            line = line[0, : n * sum(sizes)].reshape(n, 1, sum(sizes))
            line = jnp.pad(line, ((0, 0), (0, 0), (0, d - sum(sizes))))
            block = jnp.concatenate([block.reshape(n, rows, d), line], axis=1)
            block = exchange(block, rank).astype(F32)
            line = jnp.sum(block[:, rows], axis=0)
            parts = []
            at = 0
            for size in sizes:
                parts.append(line[at : at + size])
                at += size
            return block[:, :rows], parts

        grad_up, early_sums = to_owners(
            joined[units : 2 * units], joined[2 * units : 2 * units + 1], sizes
        )
        grad_w_up = grad_up.reshape(n, rows, nf, units).transpose(1, 2, 0, 3).reshape(rows, -1)
        grad_qkv, late_sums = to_owners(tail[: n * rows], tail[filled : filled + 1], late)
        grad_w_qkv = (
            grad_qkv[:, :, :wide].reshape(n, rows, 3, width).transpose(1, 2, 0, 3).reshape(rows, -1)
        )
        grads = [late_sums[0]] + early_sums[:3] + late_sums[1:] + early_sums[3:]

        x = tok.astype(F32)
        held = []

        def between(passed):
            (mixed_here, mlp_here), _ = lax.optimization_barrier(((mixed_own, mlp_parts), passed))
            out = x + bias_ends
            for k in range(n):
                out = out + nn(mixed_here[k], out_blocks[k]) + mlp_here[k].astype(F32)
            held.append(out)

        grad_q = scatter_ring([grad_q[k] for k in range(n)], between)
        block_out = held[0]
        hat, spread = normalized(x)
        grad_tokens = cot_float + spread * (
            grad_q
            - jnp.mean(grad_q, axis=-1, keepdims=True)
            - hat * jnp.mean(grad_q * hat, axis=-1, keepdims=True)
        )

        return (
            block_out.astype(BF).reshape(tokens.shape),
            grad_tokens.astype(BF).reshape(tokens.shape),
            grad_w_qkv,
            grads[0],
            grad_w_out,
            grads[1],
            grad_w_up,
            grads[2],
            grad_w_down,
            grads[3],
            grads[4],
            grads[5],
            grads[6],
            grads[7],
        )

    return body


def solution(mesh):
    tok = P("fsdp", "seq", None)
    mat = P(("fsdp", "seq"), None)
    vec = P(("fsdp", "seq"))
    params = (mat, vec, mat, vec, mat, vec, mat, vec, vec, vec, vec, vec)
    return jax.shard_map(
        make_body(mesh.shape["fsdp"], mesh.shape["seq"]),
        mesh=mesh,
        in_specs=(tok, tok) + params,
        out_specs=(tok, tok) + params,
        check_vma=False,
    )
```

```python
import math

import jax
import jax.numpy as jnp
from jax import lax
from jax.experimental import pallas as pl
from jax.experimental.pallas import tpu as pltpu
from jax.sharding import PartitionSpec as P

HEAD = 64
ROT = 16
mask_fill = -1e30
eps = 1e-05
BLK = 256
F32 = jnp.float32
BF = jnp.bfloat16


def rot_tables(positions):
    lane = lax.broadcasted_iota(jnp.int32, (1, 128), 1) % HEAD
    half = ROT // 2
    inv = jnp.exp((lane % half).astype(F32) * (-2.0 * math.log(10000.0) / ROT))
    ang = positions.astype(F32)[:, None] * inv
    cos, sin = jnp.cos(ang), jnp.sin(ang)
    c = jnp.where(lane < ROT, cos, 1.0)
    sa = jnp.where(lane < half, -sin, 0.0)
    sb = jnp.where((lane >= half) & (lane < ROT), sin, 0.0)
    return c, sa, sb

def nt(a, b):
    return lax.dot_general(a, b, (((1,), (1,)), ((), ())), preferred_element_type=F32)

def nn(a, b):
    return lax.dot_general(a, b, (((1,), (0,)), ((), ())), preferred_element_type=F32)

def attend(rank, proj, grad_mixed, tables):
    n, c, width = grad_mixed.shape
    heads = width // HEAD
    length = n * c
    half = ROT // 2
    nq = length // BLK
    scale = HEAD ** (-0.5)

    def kernel(rank_ref, proj_ref, gm_ref, c_ref, sa_ref, sb_ref, mixed_ref, gp_ref, sum_ref,
               q_s, k_s, v_s, d_s, dk_s, dv_s, s_s, dp_s, p_s):
        rank = rank_ref[0]

        def spin(x, at, sign):
            cc, sa, sb = c_ref[at], sa_ref[at], sb_ref[at]
            left = pltpu.roll(x, 128 - half, 1)
            right = pltpu.roll(x, half, 1)
            return x * cc + sign * (left * sa + right * sb)

        def load(chunk, carry):
            at = lax.rem(rank - chunk + n, n)
            rows = pl.ds(pl.multiple_of(chunk * c, c), c)
            for tile in range(2 * width // 128):
                x = spin(proj_ref[at, :, tile * 128:(tile + 1) * 128], at, 1.0)
                for side in range(2):
                    slot = tile * 2 + side
                    piece = x[:, side * HEAD:(side + 1) * HEAD].astype(BF)
                    if slot < heads:
                        q_s[slot, rows, :] = piece * jnp.asarray(scale, BF)
                    else:
                        k_s[slot - heads, rows, :] = piece
            for h in range(heads):
                v_s[h, rows, :] = proj_ref[at, :, 2 * width + h * HEAD:2 * width + (h + 1) * HEAD].astype(BF)
                d_s[h, rows, :] = gm_ref[at, :, h * HEAD:(h + 1) * HEAD]
            return carry
        lax.fori_loop(0, n, load, 0)

        def one_head(h, carry):
            dk_s[h] = jnp.zeros((length, HEAD), F32)
            dv_s[h] = jnp.zeros((length, HEAD), F32)
            row = lax.broadcasted_iota(jnp.int32, (BLK, BLK), 0)
            col = lax.broadcasted_iota(jnp.int32, (BLK, BLK), 1)
            tri = row <= col
            for i in range(nq):
                span = slice(i * BLK, (i + 1) * BLK)
                qi = q_s[h, span, :]
                di = d_s[h, span, :]
                top = jnp.full((8, BLK), mask_fill, F32)
                for j in range(i + 1):
                    s = nt(k_s[h, j * BLK:(j + 1) * BLK, :], qi)
                    if j == i:
                        s = jnp.where(tri, s, mask_fill)
                    s_s[j] = s
                    top = jnp.maximum(top, jnp.max(s.reshape(BLK // 8, 8, BLK), axis=0))
                top = jnp.max(top, axis=0, keepdims=True)
                tot = jnp.zeros((8, BLK), F32)
                for j in range(i + 1):
                    e = jnp.exp(s_s[j] - top)
                    s_s[j] = e
                    tot = tot + jnp.sum(e.reshape(BLK // 8, 8, BLK), axis=0)
                inv = 1.0 / jnp.sum(tot, axis=0, keepdims=True)
                out = jnp.zeros((HEAD, BLK), F32)
                delta = jnp.zeros((8, BLK), F32)
                for j in range(i + 1):
                    keys = slice(j * BLK, (j + 1) * BLK)
                    p = s_s[j] * inv
                    s_s[j] = p
                    low = p.astype(BF)
                    dp = nt(v_s[h, keys, :], di)
                    dp_s[j] = dp
                    delta = delta + jnp.sum((p * dp).reshape(BLK // 8, 8, BLK), axis=0)
                    out = out + nn(v_s[h, keys, :].T, low)
                    dv_s[h, keys, :] = dv_s[h, keys, :] + nn(low, di)
                delta = jnp.sum(delta, axis=0, keepdims=True)
                dq = jnp.zeros((HEAD, BLK), F32)
                for j in range(i + 1):
                    keys = slice(j * BLK, (j + 1) * BLK)
                    ds = (s_s[j] * (dp_s[j] - delta)).astype(BF)
                    dq = dq + nn(k_s[h, keys, :].T, ds)
                    dk_s[h, keys, :] = dk_s[h, keys, :] + nn(ds, qi)
                q_s[h, span, :] = (dq * scale).T.astype(BF)
                d_s[h, span, :] = out.T.astype(BF)
            return carry
        lax.fori_loop(0, heads, one_head, 0)

        sum_ref[...] = jnp.zeros_like(sum_ref)

        def store(chunk, carry):
            at = lax.rem(rank - chunk + n, n)
            rows = pl.ds(pl.multiple_of(chunk * c, c), c)
            for tile in range(2 * width // 128):
                pieces = []
                for side in range(2):
                    slot = tile * 2 + side
                    if slot < heads:
                        pieces.append(q_s[slot, rows, :].astype(F32))
                    else:
                        pieces.append(dk_s[slot - heads, rows, :].astype(BF).astype(F32))
                x = spin(jnp.concatenate(pieces, axis=1), at, -1.0).astype(BF)
                lanes = slice(tile * 128, (tile + 1) * 128)
                gp_ref[at, :, lanes] = x
                sum_ref[:, lanes] += jnp.sum(x.astype(F32).reshape(c // 8, 8, 128), axis=0)
            x = jnp.concatenate([dv_s[h, rows, :].astype(BF) for h in range(heads)], axis=1)
            gp_ref[at, :, 2 * width:] = x
            sum_ref[:, 2 * width:] += jnp.sum(x.astype(F32).reshape(c // 8, 8, width), axis=0)
            mixed_ref[at] = jnp.concatenate([d_s[h, rows, :] for h in range(heads)], axis=1)
            return carry
        lax.fori_loop(0, n, store, 0)

    vm = pl.BlockSpec(memory_space=pltpu.VMEM)
    flops = 6 * heads * length * length * HEAD
    return pl.pallas_call(
        kernel,
        out_shape=(
            jax.ShapeDtypeStruct((n, c, width), BF),
            jax.ShapeDtypeStruct((n, c, 3 * width), BF),
            jax.ShapeDtypeStruct((8, 3 * width), F32),
        ),
        in_specs=[pl.BlockSpec(memory_space=pltpu.SMEM)] + [vm] * 5,
        out_specs=(vm, vm, vm),
        scratch_shapes=[pltpu.VMEM((heads, length, HEAD), BF)] * 4
        + [pltpu.VMEM((heads, length, HEAD), F32)] * 2
        + [pltpu.VMEM((nq, BLK, BLK), F32)] * 2 + [pltpu.VMEM((8, 128), BF)],
        compiler_params=pltpu.CompilerParams(vmem_limit_bytes=56 << 20),
        cost_estimate=pl.CostEstimate(flops=flops, bytes_accessed=16 << 20, transcendentals=heads * length * length // 2),
        name="attend",
    )(rank, proj, grad_mixed, *tables)


def tn(a, b):
    return lax.dot_general(a, b, (((0,), (0,)), ((), ())), preferred_element_type=F32)


def normalized(x):
    centred = x - jnp.mean(x, axis=-1, keepdims=True)
    spread = lax.rsqrt(jnp.mean(centred * centred, axis=-1, keepdims=True) + eps)
    return centred * spread, spread


def half_erf(pre):
    return 0.5 * (1.0 + lax.erf(pre * math.sqrt(0.5)))


def tokens_spec(size):
    return pl.BlockSpec((None, BLK, size), lambda i, j, *_: (i, j, 0))


def whole_spec(shape):
    return pl.BlockSpec(shape, lambda i, j, *_: (0,) * len(shape))


def rows8(v):
    return jnp.sum(v.reshape(BLK // 8, 8, v.shape[1]), axis=0)


def spread_out(ref, totals, nf):
    tall, d = ref.shape[1:]
    for f in range(nf):
        at = 0
        for total in totals:
            size, wide = total.shape[0] // nf, total.shape[1]
            ref[f, at : at + size, :wide] = total[f * size : (f + 1) * size, :].astype(BF)
            if wide < d:
                ref[f, at : at + size, wide:] = jnp.zeros((size, d - wide), BF)
            at += size
        if at < tall:
            ref[f, at:, :] = jnp.zeros((tall - at, d), BF)


def feed(nf, spare, rank, toks, cots, norms, weights, b_qkv, w_out, b_up):
    n, c, d = toks.shape
    wide, width, hid = b_qkv.shape[1], w_out.shape[0], b_up.shape[1]
    last = n * (c // BLK) - 1
    tall = (d + hid) // nf + spare

    def kernel(
        rank_ref, x_ref, cot_ref, norm_ref, w_ref, bq_ref, wo_ref, bu_ref,
        proj_ref, mixed_ref, out_ref, q_ref, all_ref, sum_ref, up_ref, au, ad,
    ):
        w_up = w_ref[:, :hid]
        w_down = w_ref[:, hid : hid + d]
        w_qkv = w_ref[:, hid + d :]
        step = pl.program_id(0) * (c // BLK) + pl.program_id(1)

        @pl.when(step == 0)
        def _():
            for ref in (au, ad, sum_ref, up_ref):
                ref[...] = jnp.zeros_like(ref)

        hat, _ = normalized(x_ref[...].astype(F32))
        one = (hat * norm_ref[0:1] + norm_ref[1:2]).astype(BF)
        two = (hat * norm_ref[2:3] + norm_ref[3:4]).astype(BF)
        cot = cot_ref[...]
        proj_ref[...] = nn(one, w_qkv) + bq_ref[...]
        mixed_ref[...] = nt(cot, wo_ref[...]).astype(BF)
        pre = nn(two, w_up) + bu_ref[...]
        bell = half_erf(pre)
        hidden = (pre * bell).astype(BF)
        out_ref[...] = nn(hidden, w_down).astype(BF)
        slope = bell + pre * jnp.exp(-0.5 * pre * pre) * (1.0 / math.sqrt(2.0 * math.pi))
        grad_pre = (nt(cot, w_down) * slope).astype(BF)
        arriving = nt(grad_pre, w_up)
        q_ref[...] = (arriving * norm_ref[2:3]).astype(BF)
        sum_ref[0] += rows8(arriving * hat)
        sum_ref[1] += rows8(arriving)
        up_ref[...] += rows8(grad_pre.astype(F32))
        ad[...] += tn(hidden, cot)
        au[...] += tn(two, grad_pre)

        @pl.when(step == last)
        def _():
            spread_out(all_ref, (ad, au), nf)

    ins = (toks, cots, norms, weights, b_qkv, w_out, b_up)
    return pl.pallas_call(
        kernel,
        grid_spec=pltpu.PrefetchScalarGridSpec(
            num_scalar_prefetch=1,
            grid=(n, c // BLK),
            in_specs=[tokens_spec(d)] * 2 + [whole_spec(a.shape) for a in ins[2:]],
            out_specs=(
                tokens_spec(wide), tokens_spec(width),
                pl.BlockSpec((None, BLK, d), lambda i, j, r: (lax.rem(r[0] - i + n, n), j, 0)),
                tokens_spec(d),
                whole_spec((nf, tall, d)), whole_spec((2, 8, d)), whole_spec((8, hid)),
            ),
            scratch_shapes=[pltpu.VMEM((d, hid), F32), pltpu.VMEM((hid, d), F32)],
        ),
        out_shape=(
            jax.ShapeDtypeStruct((n, c, wide), F32),
            jax.ShapeDtypeStruct((n, c, width), BF),
            jax.ShapeDtypeStruct((n, c, d), BF),
            jax.ShapeDtypeStruct((n, c, d), BF),
            jax.ShapeDtypeStruct((nf, tall, d), BF),
            jax.ShapeDtypeStruct((2, 8, d), F32),
            jax.ShapeDtypeStruct((8, hid), F32),
        ),
        compiler_params=pltpu.CompilerParams(vmem_limit_bytes=60 << 20),
        cost_estimate=pl.CostEstimate(
            flops=2 * n * c * d * (wide + width + 6 * hid), bytes_accessed=30 << 20,
            transcendentals=2 * n * c * hid,
        ),
        name="feed",
    )(rank, *ins)


def finish(nf, tall, toks, cots, rest, grad_proj, mixed, norms, weights):
    n, c, d = toks.shape
    wide, width = grad_proj.shape[2], mixed.shape[2]
    last = n * (c // BLK) - 1

    def kernel(
        x_ref, cot_ref, rest_ref, gp_ref, mixed_ref, norm_ref, wq_ref,
        q_ref, all_ref, sum_ref, aq, ao,
    ):
        step = pl.program_id(0) * (c // BLK) + pl.program_id(1)

        @pl.when(step == 0)
        def _():
            for ref in (aq, ao, sum_ref):
                ref[...] = jnp.zeros_like(ref)

        hat, _ = normalized(x_ref[...].astype(F32))
        one = (hat * norm_ref[0:1] + norm_ref[1:2]).astype(BF)
        grad_proj = gp_ref[...]
        arriving = nt(grad_proj, wq_ref[:, wq_ref.shape[1] - wide :])
        q_ref[...] = (arriving * norm_ref[0:1] + rest_ref[...].astype(F32)).astype(BF)
        sum_ref[0] += rows8(arriving * hat)
        sum_ref[1] += rows8(arriving)
        aq[...] += tn(one, grad_proj)
        ao[...] += tn(mixed_ref[...], cot_ref[...])

        @pl.when(step == last)
        def _():
            spread_out(all_ref, (aq, ao), nf)

    ins = (toks, cots, rest, grad_proj, mixed, norms, weights)
    return pl.pallas_call(
        kernel,
        grid=(n, c // BLK),
        in_specs=[tokens_spec(a.shape[2]) for a in ins[:5]] + [whole_spec(a.shape) for a in ins[5:]],
        out_specs=(tokens_spec(d), whole_spec((nf, tall, d)), whole_spec((2, 8, d))),
        out_shape=(
            jax.ShapeDtypeStruct((n, c, d), BF),
            jax.ShapeDtypeStruct((nf, tall, d), BF),
            jax.ShapeDtypeStruct((2, 8, d), F32),
        ),
        scratch_shapes=[pltpu.VMEM((d, wide), F32), pltpu.VMEM((width, d), F32)],
        compiler_params=pltpu.CompilerParams(vmem_limit_bytes=60 << 20),
        cost_estimate=pl.CostEstimate(
            flops=n * c * d, bytes_accessed=n * c * d, transcendentals=0
        ),
        name="finish",
    )(*ins)


def make_body(nf, n):
    both = ("fsdp", "seq")

    def send(x, k):
        return lax.ppermute(x, "seq", [(i, (i + k) % n) for i in range(n)])

    def hop(x, pairs):
        return lax.ppermute(x, "seq", pairs)

    def gather_ring(x, rank, between):
        right, left = [x], [x]
        for t in range(1, n):
            right[-1], left[-1] = between(t, (right[-1], left[-1]))
            right.append(hop(right[-1], [(i, i + 1) for i in range(t - 1, n - 1)]))
            left.append(hop(left[-1], [(i, i - 1) for i in range(1, n - t + 1)]))
        return [x] + [jnp.where(rank >= k, right[k], left[n - k]) for k in range(1, n)]

    def scatter_ring(parts, between):
        right = left = None
        for t in range(1, n):
            if t == n - 1:
                between((right, left))
            rising = parts[t] if right is None else parts[t].astype(F32) + right.astype(F32)
            falling = parts[n - t] if left is None else parts[n - t].astype(F32) + left.astype(F32)
            right = hop(rising.astype(BF), [(i, i + 1) for i in range(t)])
            left = hop(falling.astype(BF), [(i, i - 1) for i in range(n - t, n)])
        return parts[0].astype(F32) + (right.astype(F32) + left.astype(F32))

    def in_order(parts, rank):
        out = jnp.zeros((n,) + parts[0].shape, parts[0].dtype)
        for k in range(n):
            out = lax.dynamic_update_index_in_dim(out, parts[k], (rank - k) % n, 0)
        return out

    def exchange(blocks, rank):
        own = [lax.dynamic_index_in_dim(blocks, (rank + k) % n, 0, keepdims=False) for k in range(n)]
        return in_order([send(own[k], k) if k else own[k] for k in range(n)], rank)

    def body(
        tokens,
        cotangent,
        w_qkv,
        b_qkv,
        w_out,
        b_out,
        w_up,
        b_up,
        w_down,
        b_down,
        gain_attn,
        shift_attn,
        gain_mlp,
        shift_mlp,
    ):
        rank = lax.axis_index("seq")
        _, c, d = tokens.shape
        rows = w_qkv.shape[0]
        width = d // n
        wide = 3 * width
        units = w_down.shape[0]
        extra = 8
        while n * (rows + extra) % 16:
            extra += 1
        tok = tokens.reshape(c, d)
        cot = cotangent.reshape(c, d)

        vectors = (b_qkv, b_out, b_up, b_down, gain_attn, shift_attn, gain_mlp, shift_mlp)
        lengths = [v.shape[0] for v in vectors]
        total = sum(lengths)
        pack = jnp.stack([jnp.pad(v, (0, d - v.shape[0])) for v in vectors])
        same = jnp.concatenate([w_out, pack, jnp.zeros((extra - len(vectors), d), BF)])
        qkv_cols = w_qkv.reshape(rows, 3, n, width).transpose(2, 0, 1, 3).reshape(n, rows, wide)
        up_cols = w_up.reshape(rows, nf, n, units).transpose(2, 0, 1, 3).reshape(n, rows, nf * units)
        message = jnp.concatenate(
            [
                jnp.broadcast_to(same, (n, rows + extra, d)),
                jnp.pad(up_cols, ((0, 0), (0, extra), (0, 0))),
                jnp.pad(qkv_cols, ((0, 0), (0, extra), (0, 0))),
            ],
            axis=2,
        )
        found = []

        def prepare():
            blocks = found[0].reshape(nf, n, rows + extra, d)
            full_out = blocks[:, :, :rows].reshape(d, d)
            full = [
                blocks[:, :, rows + i, :size].reshape(-1).astype(F32)
                for i, size in enumerate(lengths)
            ]
            norms = jnp.stack(full[4:] + [jnp.zeros((d,), F32)] * 4)
            own_bias_qkv = lax.dynamic_index_in_dim(full[0].reshape(3, n, width), rank, 1)
            own_bias_up = lax.dynamic_index_in_dim(full[2].reshape(nf, n, units), rank, 1)
            out_blocks = [
                lax.dynamic_slice_in_dim(full_out, (rank + k) % n * width, width, 0) for k in range(n)
            ]
            return (
                full[1] + full[3], norms, own_bias_qkv.reshape(1, -1), own_bias_up.reshape(1, -1),
                out_blocks,
            )

        def between(t, passed):
            if t == 2:
                tables = [
                    rot_tables((rank - k) % n * c + jnp.arange(c, dtype=jnp.int32)) for k in range(n)
                ]
                tables = [jnp.stack(t) for t in zip(*tables)]
                mine, tables, passed = lax.optimization_barrier((message, tables, passed))
                mine = exchange(mine, rank)
                head = mine[:, :, :d].reshape(n * (rows + extra), d)
                found.append(lax.all_gather(head, "fsdp", axis=0, tiled=True))
                side = mine[:, :rows, d:].reshape(n * rows, -1)
                hid = nf * units
                side = jnp.concatenate([side[:, :hid], w_down, side[:, hid:]], axis=1)
                found.append(lax.all_gather(side, "fsdp", axis=0, tiled=True))
                found.append(tables)
            return passed

        chunks = gather_ring(jnp.stack([tok, cot]), rank, between)
        toks = jnp.stack([pair[0] for pair in chunks])
        cots = jnp.stack([pair[1] for pair in chunks])
        _, weights, tables = found
        bias_ends, norms, own_bias_qkv, own_bias_up, out_blocks = prepare()

        def packed_row(sums, sizes):
            row = jnp.concatenate([v.reshape(nf, n, size) for v, size in zip(sums, sizes)], axis=2)
            row = row.reshape(nf, 1, n * sum(sizes)).astype(BF)
            return jnp.pad(row, ((0, 0), (0, 0), (0, d - row.shape[2])))

        def place(values, parts):
            mine = lax.broadcasted_iota(jnp.int32, (1, n, 1), 1) == rank
            return jnp.where(mine, values.reshape(parts, 1, -1), 0.0).reshape(-1)

        cot_float = cot.astype(F32)
        sum_out = jnp.sum(cot_float, axis=0)
        projected, grad_mixed, mlp_parts, rest, joined, sums_two, sum_up = feed(
            nf, -(-(2 * units + 1) // 16) * 16 - 2 * units,
            jnp.full((1,), rank, jnp.int32), toks, cots, norms, weights,
            own_bias_qkv, out_blocks[0], own_bias_up,
        )
        mlp_out = lax.psum_scatter(
            mlp_parts.reshape(n * c, d), "seq", scatter_dimension=0, tiled=True
        )
        sums_two = jnp.sum(sums_two, axis=1)
        sizes = (lengths[1], lengths[2], lengths[3], lengths[6], lengths[7])
        row = packed_row(
            (sum_out, place(jnp.sum(sum_up, axis=0), nf), sum_out, sums_two[0], sums_two[1]), sizes
        )
        joined = lax.dynamic_update_slice(joined, row, (0, 2 * units, 0))
        joined = lax.all_to_all(joined, "fsdp", split_axis=0, concat_axis=0, tiled=True)
        mixed, grad_proj, sum_qkv = attend(
            jnp.full((1,), rank, jnp.int32), projected, grad_mixed, tables
        )
        mlp_out, joined, mixed, grad_proj = lax.optimization_barrier(
            (mlp_out, joined, mixed, grad_proj)
        )
        mixed_own = [send(mixed[k], -k) if k else mixed[k] for k in range(n)]
        filled = n * rows + rows
        tall = -(-(filled + 1) // 16) * 16
        grad_q, tail, sums_one = finish(
            nf, tall, toks, cots, rest, grad_proj, mixed, norms, weights
        )
        mixed_own, grad_q = lax.optimization_barrier((mixed_own, grad_q))

        sums_one = jnp.sum(sums_one, axis=1)
        late = (lengths[0], lengths[4], lengths[5])
        row = packed_row((place(jnp.sum(sum_qkv, axis=0), 3), sums_one[0], sums_one[1]), late)
        tail = lax.dynamic_update_slice(tail, row, (0, filled, 0))
        tail = lax.psum_scatter(tail.reshape(-1, d), "fsdp", scatter_dimension=0, tiled=True)
        joined = jnp.sum(joined.astype(F32), axis=0)
        grad_w_down = joined[:units]
        joined = joined[units:].astype(BF)
        grad_w_out = lax.ppermute(
            tail[n * rows : filled],
            both,
            [(f * n + s, s * nf + f) for f in range(nf) for s in range(n)],
        ).astype(F32)

        def to_owners(block, line, sizes):
            line = line[0, : n * sum(sizes)].reshape(n, 1, sum(sizes))
            line = jnp.pad(line, ((0, 0), (0, 0), (0, d - sum(sizes))))
            block = jnp.concatenate([block.reshape(n, rows, d), line], axis=1)
            block = exchange(block, rank).astype(F32)
            line = jnp.sum(block[:, rows], axis=0)
            parts = []
            at = 0
            for size in sizes:
                parts.append(line[at : at + size])
                at += size
            return block[:, :rows], parts

        grad_up, early_sums = to_owners(
            joined[:units], joined[units : units + 1], sizes
        )
        grad_w_up = grad_up.reshape(n, rows, nf, units).transpose(1, 2, 0, 3).reshape(rows, -1)
        grad_qkv, late_sums = to_owners(tail[: n * rows], tail[filled : filled + 1], late)
        grad_w_qkv = (
            grad_qkv[:, :, :wide].reshape(n, rows, 3, width).transpose(1, 2, 0, 3).reshape(rows, -1)
        )
        grads = [late_sums[0]] + early_sums[:3] + late_sums[1:] + early_sums[3:]

        x = tok.astype(F32)
        held = []

        def between(passed):
            mixed_here, _ = lax.optimization_barrier((mixed_own, passed))
            out = x + bias_ends + mlp_out.astype(F32)
            for k in range(n):
                out = out + nn(mixed_here[k], out_blocks[k])
            held.append(out)

        grad_q = scatter_ring([grad_q[k] for k in range(n)], between)
        block_out = held[0]
        hat, spread = normalized(x)
        grad_tokens = cot_float + spread * (
            grad_q
            - jnp.mean(grad_q, axis=-1, keepdims=True)
            - hat * jnp.mean(grad_q * hat, axis=-1, keepdims=True)
        )

        return (
            block_out.astype(BF).reshape(tokens.shape),
            grad_tokens.astype(BF).reshape(tokens.shape),
            grad_w_qkv,
            grads[0],
            grad_w_out,
            grads[1],
            grad_w_up,
            grads[2],
            grad_w_down,
            grads[3],
            grads[4],
            grads[5],
            grads[6],
            grads[7],
        )

    return body


def solution(mesh):
    tok = P("fsdp", "seq", None)
    mat = P(("fsdp", "seq"), None)
    vec = P(("fsdp", "seq"))
    params = (mat, vec, mat, vec, mat, vec, mat, vec, vec, vec, vec, vec)
    return jax.shard_map(
        make_body(mesh.shape["fsdp"], mesh.shape["seq"]),
        mesh=mesh,
        in_specs=(tok, tok) + params,
        out_specs=(tok, tok) + params,
        check_vma=False,
    )
```

```python
import math

import jax
import jax.numpy as jnp
from jax import lax
from jax.experimental import pallas as pl
from jax.experimental.pallas import tpu as pltpu
from jax.sharding import PartitionSpec as P

HEAD = 64
ROT = 16
mask_fill = -1e30
eps = 1e-05
BLK = 256
TOK = 512
F32 = jnp.float32
BF = jnp.bfloat16


def rot_tables(positions):
    lane = lax.broadcasted_iota(jnp.int32, (1, 128), 1) % HEAD
    half = ROT // 2
    inv = jnp.exp((lane % half).astype(F32) * (-2.0 * math.log(10000.0) / ROT))
    ang = positions.astype(F32)[:, None] * inv
    cos, sin = jnp.cos(ang), jnp.sin(ang)
    c = jnp.where(lane < ROT, cos, 1.0)
    sa = jnp.where(lane < half, -sin, 0.0)
    sb = jnp.where((lane >= half) & (lane < ROT), sin, 0.0)
    return c, sa, sb

def nt(a, b):
    return lax.dot_general(a, b, (((1,), (1,)), ((), ())), preferred_element_type=F32)

def nn(a, b):
    return lax.dot_general(a, b, (((1,), (0,)), ((), ())), preferred_element_type=F32)

def attend(rank, proj, grad_mixed, tables):
    n, c, width = grad_mixed.shape
    heads = width // HEAD
    length = n * c
    half = ROT // 2
    nq = length // BLK
    scale = HEAD ** (-0.5)

    def kernel(rank_ref, proj_ref, gm_ref, c_ref, sa_ref, sb_ref, mixed_ref, gp_ref, sum_ref,
               q_s, k_s, v_s, d_s, dk_s, dv_s, s_s, dp_s, p_s):
        rank = rank_ref[0]

        def spin(x, at, sign):
            cc, sa, sb = c_ref[at], sa_ref[at], sb_ref[at]
            left = pltpu.roll(x, 128 - half, 1)
            right = pltpu.roll(x, half, 1)
            return x * cc + sign * (left * sa + right * sb)

        def load(chunk, carry):
            at = lax.rem(rank - chunk + n, n)
            rows = pl.ds(pl.multiple_of(chunk * c, c), c)
            for tile in range(2 * width // 128):
                x = spin(proj_ref[at, :, tile * 128:(tile + 1) * 128], at, 1.0)
                for side in range(2):
                    slot = tile * 2 + side
                    piece = x[:, side * HEAD:(side + 1) * HEAD].astype(BF)
                    if slot < heads:
                        q_s[slot, rows, :] = piece * jnp.asarray(scale, BF)
                    else:
                        k_s[slot - heads, rows, :] = piece
            for h in range(heads):
                v_s[h, rows, :] = proj_ref[at, :, 2 * width + h * HEAD:2 * width + (h + 1) * HEAD].astype(BF)
                d_s[h, rows, :] = gm_ref[at, :, h * HEAD:(h + 1) * HEAD]
            return carry
        lax.fori_loop(0, n, load, 0)

        def one_head(h, carry):
            dk_s[h] = jnp.zeros((length, HEAD), F32)
            dv_s[h] = jnp.zeros((length, HEAD), F32)
            row = lax.broadcasted_iota(jnp.int32, (BLK, BLK), 0)
            col = lax.broadcasted_iota(jnp.int32, (BLK, BLK), 1)
            tri = row <= col
            for i in range(nq):
                span = slice(i * BLK, (i + 1) * BLK)
                qi = q_s[h, span, :]
                di = d_s[h, span, :]
                top = jnp.full((8, BLK), mask_fill, F32)
                for j in range(i + 1):
                    s = nt(k_s[h, j * BLK:(j + 1) * BLK, :], qi)
                    if j == i:
                        s = jnp.where(tri, s, mask_fill)
                    s_s[j] = s
                    top = jnp.maximum(top, jnp.max(s.reshape(BLK // 8, 8, BLK), axis=0))
                top = jnp.max(top, axis=0, keepdims=True)
                tot = jnp.zeros((8, BLK), F32)
                for j in range(i + 1):
                    e = jnp.exp(s_s[j] - top)
                    s_s[j] = e
                    tot = tot + jnp.sum(e.reshape(BLK // 8, 8, BLK), axis=0)
                inv = 1.0 / jnp.sum(tot, axis=0, keepdims=True)
                out = jnp.zeros((HEAD, BLK), F32)
                delta = jnp.zeros((8, BLK), F32)
                for j in range(i + 1):
                    keys = slice(j * BLK, (j + 1) * BLK)
                    p = s_s[j] * inv
                    s_s[j] = p
                    low = p.astype(BF)
                    dp = nt(v_s[h, keys, :], di)
                    dp_s[j] = dp
                    delta = delta + jnp.sum((p * dp).reshape(BLK // 8, 8, BLK), axis=0)
                    out = out + nn(v_s[h, keys, :].T, low)
                    dv_s[h, keys, :] = dv_s[h, keys, :] + nn(low, di)
                delta = jnp.sum(delta, axis=0, keepdims=True)
                dq = jnp.zeros((HEAD, BLK), F32)
                for j in range(i + 1):
                    keys = slice(j * BLK, (j + 1) * BLK)
                    ds = (s_s[j] * (dp_s[j] - delta)).astype(BF)
                    dq = dq + nn(k_s[h, keys, :].T, ds)
                    dk_s[h, keys, :] = dk_s[h, keys, :] + nn(ds, qi)
                q_s[h, span, :] = (dq * scale).T.astype(BF)
                d_s[h, span, :] = out.T.astype(BF)
            return carry
        lax.fori_loop(0, heads, one_head, 0)

        sum_ref[...] = jnp.zeros_like(sum_ref)

        def store(chunk, carry):
            at = lax.rem(rank - chunk + n, n)
            rows = pl.ds(pl.multiple_of(chunk * c, c), c)
            for tile in range(2 * width // 128):
                pieces = []
                for side in range(2):
                    slot = tile * 2 + side
                    if slot < heads:
                        pieces.append(q_s[slot, rows, :].astype(F32))
                    else:
                        pieces.append(dk_s[slot - heads, rows, :].astype(BF).astype(F32))
                x = spin(jnp.concatenate(pieces, axis=1), at, -1.0).astype(BF)
                lanes = slice(tile * 128, (tile + 1) * 128)
                gp_ref[at, :, lanes] = x
                sum_ref[:, lanes] += jnp.sum(x.astype(F32).reshape(c // 8, 8, 128), axis=0)
            x = jnp.concatenate([dv_s[h, rows, :].astype(BF) for h in range(heads)], axis=1)
            gp_ref[at, :, 2 * width:] = x
            sum_ref[:, 2 * width:] += jnp.sum(x.astype(F32).reshape(c // 8, 8, width), axis=0)
            mixed_ref[at] = jnp.concatenate([d_s[h, rows, :] for h in range(heads)], axis=1)
            return carry
        lax.fori_loop(0, n, store, 0)

    vm = pl.BlockSpec(memory_space=pltpu.VMEM)
    flops = 6 * heads * length * length * HEAD
    return pl.pallas_call(
        kernel,
        out_shape=(
            jax.ShapeDtypeStruct((n, c, width), BF),
            jax.ShapeDtypeStruct((n, c, 3 * width), BF),
            jax.ShapeDtypeStruct((8, 3 * width), F32),
        ),
        in_specs=[pl.BlockSpec(memory_space=pltpu.SMEM)] + [vm] * 5,
        out_specs=(vm, vm, vm),
        scratch_shapes=[pltpu.VMEM((heads, length, HEAD), BF)] * 4
        + [pltpu.VMEM((heads, length, HEAD), F32)] * 2
        + [pltpu.VMEM((nq, BLK, BLK), F32)] * 2 + [pltpu.VMEM((8, 128), BF)],
        compiler_params=pltpu.CompilerParams(vmem_limit_bytes=56 << 20),
        cost_estimate=pl.CostEstimate(flops=flops, bytes_accessed=16 << 20, transcendentals=heads * length * length // 2),
        name="attend",
    )(rank, proj, grad_mixed, *tables)


def tn(a, b):
    return lax.dot_general(a, b, (((0,), (0,)), ((), ())), preferred_element_type=F32)


def normalized(x):
    centred = x - jnp.mean(x, axis=-1, keepdims=True)
    spread = lax.rsqrt(jnp.mean(centred * centred, axis=-1, keepdims=True) + eps)
    return centred * spread, spread


def half_erf(pre):
    return 0.5 * (1.0 + lax.erf(pre * math.sqrt(0.5)))


def tokens_spec(size):
    return pl.BlockSpec((None, TOK, size), lambda i, j, *_: (i, j, 0))


def whole_spec(shape):
    return pl.BlockSpec(shape, lambda i, j, *_: (0,) * len(shape))


def rows8(v):
    return jnp.sum(v.reshape(TOK // 8, 8, v.shape[1]), axis=0)


def spread_out(ref, totals, nf):
    tall, d = ref.shape[1:]
    for f in range(nf):
        at = 0
        for total in totals:
            size, wide = total.shape[0] // nf, total.shape[1]
            ref[f, at : at + size, :wide] = total[f * size : (f + 1) * size, :].astype(BF)
            if wide < d:
                ref[f, at : at + size, wide:] = jnp.zeros((size, d - wide), BF)
            at += size
        if at < tall:
            ref[f, at:, :] = jnp.zeros((tall - at, d), BF)


def feed(nf, spare, rank, toks, cots, norms, weights, b_qkv, w_out, b_up):
    n, c, d = toks.shape
    wide, width, hid = b_qkv.shape[1], w_out.shape[0], b_up.shape[1]
    last = n * (c // TOK) - 1
    tall = (d + hid) // nf + spare

    def kernel(
        rank_ref, x_ref, cot_ref, norm_ref, w_ref, bq_ref, wo_ref, bu_ref,
        proj_ref, mixed_ref, out_ref, q_ref, all_ref, sum_ref, up_ref, au, ad,
    ):
        w_up = w_ref[:, :hid]
        w_down = w_ref[:, hid : hid + d]
        w_qkv = w_ref[:, hid + d :]
        step = pl.program_id(0) * (c // TOK) + pl.program_id(1)

        @pl.when(step == 0)
        def _():
            for ref in (au, ad, sum_ref, up_ref):
                ref[...] = jnp.zeros_like(ref)

        hat, _ = normalized(x_ref[...].astype(F32))
        one = (hat * norm_ref[0:1] + norm_ref[1:2]).astype(BF)
        two = (hat * norm_ref[2:3] + norm_ref[3:4]).astype(BF)
        cot = cot_ref[...]
        proj_ref[...] = nn(one, w_qkv) + bq_ref[...]
        mixed_ref[...] = nt(cot, wo_ref[...]).astype(BF)
        pre = nn(two, w_up) + bu_ref[...]
        bell = half_erf(pre)
        hidden = (pre * bell).astype(BF)
        out_ref[...] = nn(hidden, w_down).astype(BF)
        slope = bell + pre * jnp.exp(-0.5 * pre * pre) * (1.0 / math.sqrt(2.0 * math.pi))
        grad_pre = (nt(cot, w_down) * slope).astype(BF)
        arriving = nt(grad_pre, w_up)
        q_ref[...] = (arriving * norm_ref[2:3]).astype(BF)
        sum_ref[0] += rows8(arriving * hat)
        sum_ref[1] += rows8(arriving)
        up_ref[...] += rows8(grad_pre.astype(F32))
        ad[...] += tn(hidden, cot)
        au[...] += tn(two, grad_pre)

        @pl.when(step == last)
        def _():
            spread_out(all_ref, (ad, au), nf)

    ins = (toks, cots, norms, weights, b_qkv, w_out, b_up)
    return pl.pallas_call(
        kernel,
        grid_spec=pltpu.PrefetchScalarGridSpec(
            num_scalar_prefetch=1,
            grid=(n, c // TOK),
            in_specs=[tokens_spec(d)] * 2 + [whole_spec(a.shape) for a in ins[2:]],
            out_specs=(
                tokens_spec(wide), tokens_spec(width),
                pl.BlockSpec((None, TOK, d), lambda i, j, r: (lax.rem(r[0] - i + n, n), j, 0)),
                tokens_spec(d),
                whole_spec((nf, tall, d)), whole_spec((2, 8, d)), whole_spec((8, hid)),
            ),
            scratch_shapes=[pltpu.VMEM((d, hid), F32), pltpu.VMEM((hid, d), F32)],
        ),
        out_shape=(
            jax.ShapeDtypeStruct((n, c, wide), F32),
            jax.ShapeDtypeStruct((n, c, width), BF),
            jax.ShapeDtypeStruct((n, c, d), BF),
            jax.ShapeDtypeStruct((n, c, d), BF),
            jax.ShapeDtypeStruct((nf, tall, d), BF),
            jax.ShapeDtypeStruct((2, 8, d), F32),
            jax.ShapeDtypeStruct((8, hid), F32),
        ),
        compiler_params=pltpu.CompilerParams(vmem_limit_bytes=60 << 20),
        cost_estimate=pl.CostEstimate(
            flops=2 * n * c * d * (wide + width + 6 * hid), bytes_accessed=30 << 20,
            transcendentals=2 * n * c * hid,
        ),
        name="feed",
    )(rank, *ins)


def finish(nf, tall, toks, cots, rest, grad_proj, mixed, norms, weights):
    n, c, d = toks.shape
    wide, width = grad_proj.shape[2], mixed.shape[2]
    last = n * (c // TOK) - 1

    def kernel(
        x_ref, cot_ref, rest_ref, gp_ref, mixed_ref, norm_ref, wq_ref,
        q_ref, all_ref, sum_ref, aq, ao,
    ):
        step = pl.program_id(0) * (c // TOK) + pl.program_id(1)

        @pl.when(step == 0)
        def _():
            for ref in (aq, ao, sum_ref):
                ref[...] = jnp.zeros_like(ref)

        hat, _ = normalized(x_ref[...].astype(F32))
        one = (hat * norm_ref[0:1] + norm_ref[1:2]).astype(BF)
        grad_proj = gp_ref[...]
        arriving = nt(grad_proj, wq_ref[:, wq_ref.shape[1] - wide :])
        q_ref[...] = (arriving * norm_ref[0:1] + rest_ref[...].astype(F32)).astype(BF)
        sum_ref[0] += rows8(arriving * hat)
        sum_ref[1] += rows8(arriving)
        aq[...] += tn(one, grad_proj)
        ao[...] += tn(mixed_ref[...], cot_ref[...])

        @pl.when(step == last)
        def _():
            spread_out(all_ref, (aq, ao), nf)

    ins = (toks, cots, rest, grad_proj, mixed, norms, weights)
    return pl.pallas_call(
        kernel,
        grid=(n, c // TOK),
        in_specs=[tokens_spec(a.shape[2]) for a in ins[:5]] + [whole_spec(a.shape) for a in ins[5:]],
        out_specs=(tokens_spec(d), whole_spec((nf, tall, d)), whole_spec((2, 8, d))),
        out_shape=(
            jax.ShapeDtypeStruct((n, c, d), BF),
            jax.ShapeDtypeStruct((nf, tall, d), BF),
            jax.ShapeDtypeStruct((2, 8, d), F32),
        ),
        scratch_shapes=[pltpu.VMEM((d, wide), F32), pltpu.VMEM((width, d), F32)],
        compiler_params=pltpu.CompilerParams(vmem_limit_bytes=60 << 20),
        cost_estimate=pl.CostEstimate(
            flops=n * c * d, bytes_accessed=n * c * d, transcendentals=0
        ),
        name="finish",
    )(*ins)


def make_body(nf, n):
    both = ("fsdp", "seq")

    def send(x, k):
        return lax.ppermute(x, "seq", [(i, (i + k) % n) for i in range(n)])

    def hop(x, pairs):
        return lax.ppermute(x, "seq", pairs)

    def gather_ring(x, rank, between):
        right, left = [x], [x]
        for t in range(1, n):
            right[-1], left[-1] = between(t, (right[-1], left[-1]))
            right.append(hop(right[-1], [(i, i + 1) for i in range(t - 1, n - 1)]))
            left.append(hop(left[-1], [(i, i - 1) for i in range(1, n - t + 1)]))
        return [x] + [jnp.where(rank >= k, right[k], left[n - k]) for k in range(1, n)]

    def scatter_ring(parts, between):
        right = left = None
        for t in range(1, n):
            if t == n - 1:
                between((right, left))
            rising = parts[t] if right is None else parts[t].astype(F32) + right.astype(F32)
            falling = parts[n - t] if left is None else parts[n - t].astype(F32) + left.astype(F32)
            right = hop(rising.astype(BF), [(i, i + 1) for i in range(t)])
            left = hop(falling.astype(BF), [(i, i - 1) for i in range(n - t, n)])
        return parts[0].astype(F32) + (right.astype(F32) + left.astype(F32))

    def in_order(parts, rank):
        out = jnp.zeros((n,) + parts[0].shape, parts[0].dtype)
        for k in range(n):
            out = lax.dynamic_update_index_in_dim(out, parts[k], (rank - k) % n, 0)
        return out

    def exchange(blocks, rank):
        own = [lax.dynamic_index_in_dim(blocks, (rank + k) % n, 0, keepdims=False) for k in range(n)]
        return in_order([send(own[k], k) if k else own[k] for k in range(n)], rank)

    def body(
        tokens,
        cotangent,
        w_qkv,
        b_qkv,
        w_out,
        b_out,
        w_up,
        b_up,
        w_down,
        b_down,
        gain_attn,
        shift_attn,
        gain_mlp,
        shift_mlp,
    ):
        rank = lax.axis_index("seq")
        _, c, d = tokens.shape
        rows = w_qkv.shape[0]
        width = d // n
        wide = 3 * width
        units = w_down.shape[0]
        extra = 8
        while n * (rows + extra) % 16:
            extra += 1
        tok = tokens.reshape(c, d)
        cot = cotangent.reshape(c, d)

        vectors = (b_qkv, b_out, b_up, b_down, gain_attn, shift_attn, gain_mlp, shift_mlp)
        lengths = [v.shape[0] for v in vectors]
        total = sum(lengths)
        pack = jnp.stack([jnp.pad(v, (0, d - v.shape[0])) for v in vectors])
        same = jnp.concatenate([w_out, pack, jnp.zeros((extra - len(vectors), d), BF)])
        qkv_cols = w_qkv.reshape(rows, 3, n, width).transpose(2, 0, 1, 3).reshape(n, rows, wide)
        up_cols = w_up.reshape(rows, nf, n, units).transpose(2, 0, 1, 3).reshape(n, rows, nf * units)
        message = jnp.concatenate(
            [
                jnp.broadcast_to(same, (n, rows + extra, d)),
                jnp.pad(up_cols, ((0, 0), (0, extra), (0, 0))),
                jnp.pad(qkv_cols, ((0, 0), (0, extra), (0, 0))),
            ],
            axis=2,
        )
        found = []

        def prepare():
            blocks = found[0].reshape(nf, n, rows + extra, d)
            full_out = blocks[:, :, :rows].reshape(d, d)
            full = [
                blocks[:, :, rows + i, :size].reshape(-1).astype(F32)
                for i, size in enumerate(lengths)
            ]
            norms = jnp.stack(full[4:] + [jnp.zeros((d,), F32)] * 4)
            own_bias_qkv = lax.dynamic_index_in_dim(full[0].reshape(3, n, width), rank, 1)
            own_bias_up = lax.dynamic_index_in_dim(full[2].reshape(nf, n, units), rank, 1)
            out_blocks = [
                lax.dynamic_slice_in_dim(full_out, (rank + k) % n * width, width, 0) for k in range(n)
            ]
            return (
                full[1] + full[3], norms, own_bias_qkv.reshape(1, -1), own_bias_up.reshape(1, -1),
                out_blocks,
            )

        def between(t, passed):
            if t == 2:
                tables = [
                    rot_tables((rank - k) % n * c + jnp.arange(c, dtype=jnp.int32)) for k in range(n)
                ]
                tables = [jnp.stack(t) for t in zip(*tables)]
                mine, tables, passed = lax.optimization_barrier((message, tables, passed))
                mine = exchange(mine, rank)
                head = mine[:, :, :d].reshape(n * (rows + extra), d)
                found.append(lax.all_gather(head, "fsdp", axis=0, tiled=True))
                side = mine[:, :rows, d:].reshape(n * rows, -1)
                hid = nf * units
                side = jnp.concatenate([side[:, :hid], w_down, side[:, hid:]], axis=1)
                found.append(lax.all_gather(side, "fsdp", axis=0, tiled=True))
                found.append(tables)
            return passed

        chunks = gather_ring(jnp.stack([tok, cot]), rank, between)
        toks = jnp.stack([pair[0] for pair in chunks])
        cots = jnp.stack([pair[1] for pair in chunks])
        _, weights, tables = found
        bias_ends, norms, own_bias_qkv, own_bias_up, out_blocks = prepare()

        def packed_row(sums, sizes):
            row = jnp.concatenate([v.reshape(nf, n, size) for v, size in zip(sums, sizes)], axis=2)
            row = row.reshape(nf, 1, n * sum(sizes)).astype(BF)
            return jnp.pad(row, ((0, 0), (0, 0), (0, d - row.shape[2])))

        def place(values, parts):
            mine = lax.broadcasted_iota(jnp.int32, (1, n, 1), 1) == rank
            return jnp.where(mine, values.reshape(parts, 1, -1), 0.0).reshape(-1)

        cot_float = cot.astype(F32)
        sum_out = jnp.sum(cot_float, axis=0)
        projected, grad_mixed, mlp_parts, rest, joined, sums_two, sum_up = feed(
            nf, -(-(2 * units + 1) // 16) * 16 - 2 * units,
            jnp.full((1,), rank, jnp.int32), toks, cots, norms, weights,
            own_bias_qkv, out_blocks[0], own_bias_up,
        )
        mlp_out = lax.psum_scatter(
            mlp_parts.reshape(n * c, d), "seq", scatter_dimension=0, tiled=True
        )
        sums_two = jnp.sum(sums_two, axis=1)
        sizes = (lengths[1], lengths[2], lengths[3], lengths[6], lengths[7])
        row = packed_row(
            (sum_out, place(jnp.sum(sum_up, axis=0), nf), sum_out, sums_two[0], sums_two[1]), sizes
        )
        joined = lax.dynamic_update_slice(joined, row, (0, 2 * units, 0))
        joined = lax.all_to_all(joined, "fsdp", split_axis=0, concat_axis=0, tiled=True)
        mixed, grad_proj, sum_qkv = attend(
            jnp.full((1,), rank, jnp.int32), projected, grad_mixed, tables
        )
        mlp_out, joined, mixed, grad_proj = lax.optimization_barrier(
            (mlp_out, joined, mixed, grad_proj)
        )
        mixed_own = [send(mixed[k], -k) if k else mixed[k] for k in range(n)]
        filled = n * rows + rows
        tall = -(-(filled + 1) // 16) * 16
        grad_q, tail, sums_one = finish(
            nf, tall, toks, cots, rest, grad_proj, mixed, norms, weights
        )
        mixed_own, grad_q = lax.optimization_barrier((mixed_own, grad_q))

        sums_one = jnp.sum(sums_one, axis=1)
        late = (lengths[0], lengths[4], lengths[5])
        row = packed_row((place(jnp.sum(sum_qkv, axis=0), 3), sums_one[0], sums_one[1]), late)
        tail = lax.dynamic_update_slice(tail, row, (0, filled, 0))
        tail = lax.psum_scatter(tail.reshape(-1, d), "fsdp", scatter_dimension=0, tiled=True)
        joined = jnp.sum(joined.astype(F32), axis=0)
        grad_w_down = joined[:units]
        joined = joined[units:].astype(BF)
        grad_w_out = lax.ppermute(
            tail[n * rows : filled],
            both,
            [(f * n + s, s * nf + f) for f in range(nf) for s in range(n)],
        ).astype(F32)

        def to_owners(block, line, sizes):
            line = line[0, : n * sum(sizes)].reshape(n, 1, sum(sizes))
            line = jnp.pad(line, ((0, 0), (0, 0), (0, d - sum(sizes))))
            block = jnp.concatenate([block.reshape(n, rows, d), line], axis=1)
            block = exchange(block, rank).astype(F32)
            line = jnp.sum(block[:, rows], axis=0)
            parts = []
            at = 0
            for size in sizes:
                parts.append(line[at : at + size])
                at += size
            return block[:, :rows], parts

        grad_up, early_sums = to_owners(
            joined[:units], joined[units : units + 1], sizes
        )
        grad_w_up = grad_up.reshape(n, rows, nf, units).transpose(1, 2, 0, 3).reshape(rows, -1)
        grad_qkv, late_sums = to_owners(tail[: n * rows], tail[filled : filled + 1], late)
        grad_w_qkv = (
            grad_qkv[:, :, :wide].reshape(n, rows, 3, width).transpose(1, 2, 0, 3).reshape(rows, -1)
        )
        grads = [late_sums[0]] + early_sums[:3] + late_sums[1:] + early_sums[3:]

        x = tok.astype(F32)
        held = []

        def between(passed):
            mixed_here, _ = lax.optimization_barrier((mixed_own, passed))
            out = x + bias_ends + mlp_out.astype(F32)
            for k in range(n):
                out = out + nn(mixed_here[k], out_blocks[k])
            held.append(out)

        grad_q = scatter_ring([grad_q[k] for k in range(n)], between)
        block_out = held[0]
        hat, spread = normalized(x)
        grad_tokens = cot_float + spread * (
            grad_q
            - jnp.mean(grad_q, axis=-1, keepdims=True)
            - hat * jnp.mean(grad_q * hat, axis=-1, keepdims=True)
        )

        return (
            block_out.astype(BF).reshape(tokens.shape),
            grad_tokens.astype(BF).reshape(tokens.shape),
            grad_w_qkv,
            grads[0],
            grad_w_out,
            grads[1],
            grad_w_up,
            grads[2],
            grad_w_down,
            grads[3],
            grads[4],
            grads[5],
            grads[6],
            grads[7],
        )

    return body


def solution(mesh):
    tok = P("fsdp", "seq", None)
    mat = P(("fsdp", "seq"), None)
    vec = P(("fsdp", "seq"))
    params = (mat, vec, mat, vec, mat, vec, mat, vec, vec, vec, vec, vec)
    return jax.shard_map(
        make_body(mesh.shape["fsdp"], mesh.shape["seq"]),
        mesh=mesh,
        in_specs=(tok, tok) + params,
        out_specs=(tok, tok) + params,
        check_vma=False,
    )
```
